512 devices in a mesh: vocab: 64 (over x, y, core), tok: 8 (over z).
Axes of the slice: x: 4, y: 8, z: 8, core: 2. Of those that a mesh axis runs over, the one named last changes fastest.
Arguments:
- hidden: bfloat16 [1024, 3584], P('tok'), may hold values from -320 to 320
- head: bfloat16 [3584, 98304], P('tok', 'vocab'), may hold values from -2 to 2
- teacher: bfloat16 [1024, 98304], P('tok', 'vocab'), may hold values from 0 to 1, as said below
- block_ids: int32 [8, 16], P('tok'), may hold values from -1 to 191, as said below
- counts: int32 [8], P('tok'), may hold values from 8 to 16
Outputs:
- lse: float32 [1024], P('tok')
- kl: float32 [1024], P('tok')
- grad_hidden: float32 [1024, 3584], P('tok', 'vocab')
- grad_head: bfloat16 [3584, 98304], P('tok', 'vocab')
The draws below stay inside these ranges and needn't reach their ends.
Inputs may be any that keep to these rules, and one draw needn't show every extreme that they name: `block_ids`: row b lists counts[b] distinct teacher blocks (block k covers columns 512 * k to 512 * k + 511) in its first counts[b] entries; the rest of the row is -1. `teacher`: every entry is positive.
All inputs are finite; a program needn't handle non-finite values.
Results may differ from the reference program's by a relative error of at most 0.0055.
Values may be sent and summed in bfloat16 or wider, within the bound.
A program may use at most 64 MiB of HBM per device.

```python
import jax
import jax.numpy as jnp
from jax import lax

D = 3584
BLK = 512
TB = 128
SLOTS = 16
V = 98304
TOKENS = 1024
NTB = 8


def shared_direction(key):
    return jax.random.rademacher(jax.random.fold_in(key, 7), (D,), dtype=jnp.float32)


def drawn_start(key):
    return jax.random.randint(jax.random.fold_in(key, 9), (), 0, V - 3)


def draw_hidden(key, part):
    return jax.random.truncated_normal(jax.random.fold_in(key, 1), -6.0, 6.0, (TOKENS, D)).astype(jnp.bfloat16)


def draw_head(key, part):
    position = jnp.arange(V, dtype=jnp.int32)
    spread = (2.9 + 0.45 * position.astype(jnp.float32) / V) / D ** 0.5
    base_values = jax.random.truncated_normal(jax.random.fold_in(key, 2), -4.0, 4.0, (D, V)) * spread[None, :]
    offset = position - drawn_start(key)
    inside = (offset >= 0) & (offset < 3)
    factor = 2.0 ** (-(D.bit_length() - 1))
    levels = (1.0 - jnp.clip(offset, 0, 2).astype(jnp.float32) * 2.0 ** (-8)) * factor
    aligned = shared_direction(key)[:, None] * levels[None, :]
    return jnp.where(inside[None, :], aligned, base_values).astype(jnp.bfloat16)


def draw_teacher(key, part):
    position = jnp.arange(V, dtype=jnp.float32) / V
    element = jax.random.uniform(jax.random.fold_in(key, 31), (TOKENS, V))
    column = jax.random.uniform(jax.random.fold_in(key, 32), (V,))
    exponent = -10.0 * element - 4.0 * column[None, :] + 1.1 * (position[None, :] - 1.0)
    return jnp.exp(exponent).astype(jnp.bfloat16)


def teacher_lists(key):
    block_total = V // BLK
    heat = jax.random.randint(jax.random.fold_in(key, 21), (block_total,), 0, 4)
    noise = jax.random.randint(jax.random.fold_in(key, 22), (NTB, block_total), 0, 4096)
    scores = (noise + heat[None, :] * 2048) * block_total + jnp.arange(block_total, dtype=jnp.int32)[None, :]
    unused, picked = lax.top_k(scores, SLOTS)
    drawn = jax.random.randint(jax.random.fold_in(key, 23), (NTB,), SLOTS // 2, SLOTS + 1)
    fullest = jax.random.randint(jax.random.fold_in(key, 24), (), 0, NTB)
    row_index = jnp.arange(NTB, dtype=jnp.int32)
    drawn = jnp.where(row_index == fullest, SLOTS, drawn)
    drawn = jnp.where(row_index == (fullest + 1) % NTB, SLOTS // 2, drawn)
    slot_index = jnp.arange(SLOTS, dtype=jnp.int32)[None, :]
    listing = jnp.where(slot_index < drawn[:, None], picked.astype(jnp.int32), -1)
    return (listing, drawn.astype(jnp.int32))


def draw_block_ids(key, part):
    return teacher_lists(key)[0]


def draw_counts(key, part):
    return teacher_lists(key)[1]


def setup_inputs(seed: int = 0) -> dict:
    key_of = jax.random.split(jax.random.key(seed), 6)
    return {
        "hidden": draw_hidden(jax.random.fold_in(key_of[5], 71), 0),
        "head": draw_head(jax.random.fold_in(key_of[5], 71), 0),
        "teacher": draw_teacher(jax.random.fold_in(key_of[5], 71), 0),
        "block_ids": draw_block_ids(jax.random.fold_in(key_of[5], 71), 0),
        "counts": draw_counts(jax.random.fold_in(key_of[5], 71), 0),
    }


loss_scale = 1024.0


def reference(hidden, head, teacher, block_ids, counts):
    logits = jnp.dot(hidden, head, preferred_element_type=jnp.float32)
    highest = jnp.max(logits, axis=1)
    lse = highest + jnp.log(jnp.sum(jnp.exp(logits - highest[:, None]), axis=1))
    block_total = head.shape[1] // BLK
    live_slot = jnp.arange(SLOTS, dtype=jnp.int32)[None, :] < counts[:, None]
    block_range = jnp.arange(block_total, dtype=jnp.int32)
    block_hit = jnp.any((block_ids[:, :, None] == block_range[None, None, :]) & live_slot[:, :, None], axis=1)
    column_hit = jnp.repeat(block_hit, BLK, axis=1)
    listed = jnp.repeat(column_hit, TB, axis=0)
    teacher_f = teacher.astype(jnp.float32)
    kept = jnp.where(listed, teacher_f, 0.0)
    mass = jnp.sum(kept, axis=1)
    weighted = jnp.sum(jnp.where(listed, teacher_f * (jnp.log(teacher_f) - logits), 0.0), axis=1)
    kl = weighted / mass - jnp.log(mass) + lse
    student = jnp.exp(logits - lse[:, None])
    delta = (loss_scale * (student - kept / mass[:, None])).astype(jnp.bfloat16)
    grad_hidden = jnp.dot(delta, head.T, preferred_element_type=jnp.float32)
    grad_head = jnp.dot(hidden.T, delta, preferred_element_type=jnp.float32).astype(jnp.bfloat16)
    return (lse, kl, grad_hidden, grad_head)
```

```python
import functools

import jax
import jax.numpy as jnp
from jax import lax
from jax.experimental import pallas as pl
from jax.experimental.pallas import tpu as pltpu
from jax.sharding import PartitionSpec as P

BLK = 512
RING_Y = 8

MESH = pl.DeviceIdType.MESH
loss_scale = 1024.0


def ring_hops(n, parts):
    if parts == 1:
        return [(n // 2, (n - 1) // 2)]
    return [(n // 2, (n - 1) // 2), ((n - 1) // 2, n // 2)]


def kernel_body(
    geo,
    hidden, head, teacher, ids, counts,
    ghead_out, ghid_out, stat_out,
    kept, hid, headt, teach, logits, stat, stat_in, delta, dg, hidt, res, gt, gc, gx, gy, gf, gsum, fin, fin_in,
    s_hz, r_hz, s_hp, r_hp, s_hd, s_hf, r_hd, s_te, r_te, s_st, r_st, s_dl, s_df, r_dl, s_ht, r_ht,
    s_gc, r_gc, s_gx, r_gx, s_gy, r_gy, s_go, r_go, s_fi, r_fi,
):
    X, Y, Z, blk = geo
    H = Z // 2
    tb, d = hidden.shape
    db, cb = head.shape
    cs = cb // H
    th = tb * H
    v = lax.axis_index("vocab")
    z = lax.axis_index("tok")
    c = lax.rem(v, 2)
    y = lax.rem(lax.div(v, 2), Y)
    x = lax.div(v, 2 * Y)
    zh, zl = lax.div(z, H), lax.rem(z, H)
    pc = 1 - c

    def dev(xx, yy, cc, zz):
        return {"vocab": (xx * Y + yy) * 2 + cc, "tok": zz}

    def rc(src, dst, ssem, rsem, device):
        return pltpu.make_async_remote_copy(
            src_ref=src, dst_ref=dst, send_sem=ssem, recv_sem=rsem, device_id=device, device_id_type=MESH
        )

    partner = dev(x, y, pc, z)
    order = sorted(range(1, Z), key=lambda o: -min(o, Z - o))

    pr, plan = tb // Y, d // X
    row0 = pl.multiple_of(y * pr, pr)
    lane0 = pl.multiple_of(x * plan, plan)
    piece = hidden.at[pl.ds(row0, pr), pl.ds(lane0, plan)]
    piece_to = hid.at[zl, pl.ds(row0, pr), pl.ds(lane0, plan)]

    def hz_copy(o):
        zd = lax.rem(z + o, Z)
        return zd, rc(piece, piece_to, s_hz.at[o], r_hz.at[zl], dev(x, y, zh, zd))

    for o in order:
        zd, copy = hz_copy(o)

        @pl.when(lax.div(zd, H) == c)
        def _():
            copy.start()

    @pl.when(zh == c)
    def _():
        pltpu.make_async_copy(piece, piece_to, r_hz.at[zl]).start()

    def hd_copy(o):
        zd = lax.rem(z + o, Z)
        cols = pl.ds(pl.multiple_of(lax.rem(zd, H) * cs, cs), cs)
        return zd, rc(head.at[:, cols], headt.at[z], s_hd.at[o], r_hd.at[z], dev(x, y, zh, zd))

    for o in order:
        zd, copy = hd_copy(o)

        @pl.when(lax.div(zd, H) == c)
        def _():
            copy.start()

    own_cols = pl.ds(pl.multiple_of(zl * cs, cs), cs)

    own_head = rc(head.at[:, own_cols], headt.at[z], s_hd.at[0], r_hd.at[z], partner)

    @pl.when(zh == c)
    def _():
        pltpu.make_async_copy(head.at[:, own_cols], headt.at[z], r_hd.at[z]).start()
        own_head.start()

    slots = ids.shape[1]
    for k in range(cb // blk):
        block = v * (cb // blk) + k
        hit = jnp.int32(0)
        for s in range(slots):
            hit = hit | jnp.where((ids[0, s] == block) & (s < counts[0]), 1, 0)
        part = teacher[:, k * blk : (k + 1) * blk]
        keep = jnp.full(part.shape, hit, jnp.int32) > 0
        kept[:, k * blk : (k + 1) * blk] = jnp.where(keep, part.astype(jnp.float32), 0.0).astype(jnp.bfloat16)

    def te_copy(o):
        zd = lax.rem(z + o, Z)
        cols = pl.ds(pl.multiple_of(lax.rem(zd, H) * cs, cs), cs)
        return zd, rc(kept.at[:, cols], teach.at[zl], s_te.at[o], r_te.at[zl], dev(x, y, zh, zd))

    for o in order:
        zd, copy = te_copy(o)

        @pl.when(lax.div(zd, H) == c)
        def _():
            copy.start()

    @pl.when(zh == c)
    def _():
        pltpu.make_async_copy(kept.at[:, own_cols], teach.at[zl], r_te.at[zl]).start()

    for k in range(H):
        pltpu.make_async_copy(piece, hid.at[k, pl.ds(row0, pr), pl.ds(lane0, plan)], r_hz.at[k]).wait()

    parts = [(0, H)] if H == 1 else [(0, H // 2), (H // 2, H // 2)]

    def ring(n, me, slot, neighbour, ssem, rsem):
        if n == 1:
            return
        hops = ring_hops(n, len(parts))

        def copy(pi, direction, s):
            index = lax.rem(me - (s - 1) + n, n) if direction == 0 else lax.rem(me + (s - 1), n)
            to = lax.rem(me + 1, n) if direction == 0 else lax.rem(me + n - 1, n)
            view = slot(index, parts[pi])
            return rc(view, view, ssem.at[pi, direction, s - 1], rsem.at[pi, direction, s - 1], neighbour(to))

        def arrived(pi, direction, s):
            index = lax.rem(me - s + n, n) if direction == 0 else lax.rem(me + s, n)
            view = slot(index, parts[pi])
            pltpu.make_async_copy(view, view, rsem.at[pi, direction, s - 1]).wait()

        for s in range(1, n // 2 + 1):
            for pi in range(len(parts)):
                for direction in range(2):
                    if s <= hops[pi][direction]:
                        if s > 1:
                            arrived(pi, direction, s - 1)
                        copy(pi, direction, s).start()
        for pi in range(len(parts)):
            for direction in range(2):
                if hops[pi][direction] > 0:
                    arrived(pi, direction, hops[pi][direction])
        for s in range(1, n // 2 + 1):
            for pi in range(len(parts)):
                for direction in range(2):
                    if s <= hops[pi][direction]:
                        copy(pi, direction, s).wait_send()

    def rows_at(i):
        return pl.ds(pl.multiple_of(i * pr, pr), pr)

    def lanes_at(i):
        return pl.ds(pl.multiple_of(i * plan, plan), plan)

    def to_x(i):
        return dev(i, y, c, z)

    def to_y(i):
        return dev(x, i, c, z)

    @pl.when(c == 0)
    def _():
        ring(X, x, lambda i, p: hid.at[pl.ds(*p), rows_at(y), lanes_at(i)], to_x, s_hp.at[0], r_hp.at[0])
        ring(Y, y, lambda i, p: hid.at[pl.ds(*p), rows_at(i), :], to_y, s_hp.at[1], r_hp.at[1])

    @pl.when(c == 1)
    def _():
        ring(Y, y, lambda i, p: hid.at[pl.ds(*p), rows_at(i), lanes_at(x)], to_y, s_hp.at[0], r_hp.at[0])
        ring(X, x, lambda i, p: hid.at[pl.ds(*p), :, lanes_at(i)], to_x, s_hp.at[1], r_hp.at[1])

    def hf_copy(zs):
        return rc(headt.at[zs], headt.at[zs], s_hf.at[lax.rem(zs, H)], r_hd.at[zs], partner)

    def head_arrived(zs):
        pltpu.make_async_copy(headt.at[zs], headt.at[zs], r_hd.at[zs]).wait()

    for o in reversed(order):
        zs = lax.rem(z + o, Z)

        @pl.when(lax.div(zs, H) == c)
        def _():
            head_arrived(zs)
            hf_copy(zs).start()

    win = hidt.shape[1]
    win0 = lax.div(z * db, 128) * 128
    off = z * db - win0
    for k in range(H):
        block = hid[k, :, pl.ds(pl.multiple_of(win0, 128), win)]
        hidt[c, :, k * tb : (k + 1) * tb] = block.T
    ht_copy = rc(hidt.at[c], hidt.at[c], s_ht, r_ht, partner)
    ht_copy.start()

    @pl.when(zh == c)
    def _():
        head_arrived(z)

    for o in reversed(order):
        zs = lax.rem(z + o, Z)

        @pl.when(lax.div(zs, H) != c)
        def _():
            head_arrived(zs)

    @pl.when(zh != c)
    def _():
        head_arrived(z)

    logits[...] = jnp.zeros_like(logits)
    kd = 2 * db

    @pl.loop(0, H)
    def _(p):
        lhs = hid[:, :, pl.ds(pl.multiple_of(p * kd, kd), kd)].reshape(th, kd)
        rhs = headt[pl.ds(2 * p, 2)].reshape(kd, cs)
        logits[...] += jnp.dot(lhs, rhs, preferred_element_type=jnp.float32)

    for k in range(H):
        pltpu.make_async_copy(teach.at[k], teach.at[k], r_te.at[k]).wait()

    lane = lax.broadcasted_iota(jnp.int32, (tb, 128), 1)

    for k in range(H):
        lk = logits[k * tb : (k + 1) * tb, :]
        tk = teach[k].astype(jnp.float32)
        top = jnp.max(lk, axis=1, keepdims=True)
        total = jnp.sum(jnp.exp(lk - top), axis=1, keepdims=True)
        mass = jnp.sum(tk, axis=1, keepdims=True)
        live = tk > 0.0
        term = jnp.where(live, tk * (jnp.log(jnp.where(live, tk, 1.0)) - lk), 0.0)
        weighted = jnp.sum(term, axis=1, keepdims=True)
        table = jnp.where(
            lane == 0, top, jnp.where(lane == 1, total, jnp.where(lane == 2, mass, weighted))
        ).T
        for q in range(4):
            stat[q * H + k : q * H + k + 1, :] = table[q : q + 1, :]

    def combine(blocks):
        tops = [b[0:H] for b in blocks]
        top = functools.reduce(jnp.maximum, tops)
        total = functools.reduce(jnp.add, [b[H : 2 * H] * jnp.exp(t - top) for b, t in zip(blocks, tops)])
        rest = functools.reduce(jnp.add, [b[2 * H :] for b in blocks])
        return top, total, rest

    def exchange(stage, n, me, to):
        if n == 1:
            return
        others = sorted(range(1, n), key=lambda o: -min(o, n - o))

        def copy(o):
            return rc(
                stat.at[...],
                stat_in.at[stage, n - o],
                s_st.at[stage, o],
                r_st.at[stage, n - o],
                to(lax.rem(me + o, n)),
            )

        for o in others:
            copy(o).start()
        for o in reversed(others):
            copy(o).wait_send()
        blocks = [stat[...]]
        for o in range(1, n):
            pltpu.make_async_copy(stat.at[...], stat_in.at[stage, o], r_st.at[stage, o]).wait()
        for o in range(1, n):
            blocks.append(stat_in[stage, o])
        top, total, rest = combine(blocks)
        stat[0:H, :] = top
        stat[H : 2 * H, :] = total
        stat[2 * H : 4 * H, :] = rest

    exchange(0, X, x, to_x)
    exchange(1, Y, y, to_y)
    exchange(2, Z, z, lambda i: dev(x, y, c, i))

    final = stat[...]
    lse = final[0:H] + jnp.log(final[H : 2 * H])
    mass = final[2 * H : 3 * H]
    kl = final[3 * H : 4 * H] / mass - jnp.log(mass) + lse
    scale = loss_scale / mass
    rows = jnp.concatenate([lse, scale, jnp.zeros((128 - 2 * H, 128), jnp.float32)], axis=0).T

    for k in range(H):
        lk = logits[k * tb : (k + 1) * tb, :]
        tk = teach[k].astype(jnp.float32)
        student = jnp.exp(lk - rows[:, k : k + 1])
        delta[k * tb : (k + 1) * tb, :] = (loss_scale * student - tk * rows[:, H + k : H + k + 1]).astype(
            jnp.bfloat16
        )

    hops = ring_hops(Z, 2)

    def dl_copy(direction):
        to = lax.rem(z + 1, Z) if direction == 0 else lax.rem(z + Z - 1, Z)
        return rc(delta.at[...], dg.at[zl, c], s_dl.at[direction], r_dl.at[zl, c], dev(x, y, zh, to))

    dl_copy(0).start()
    if hops[1][1] > 0 and hops[0][1] > 0:
        dl_copy(1).start()
    else:

        @pl.when(c == 1)
        def _():
            dl_copy(1).start()

    dl_local = rc(delta.at[...], dg.at[zl, c], s_dl.at[2], r_dl.at[zl, c], partner)

    @pl.when(zh != c)
    def _():
        dl_local.start()

    @pl.when(zh == c)
    def _():
        pltpu.make_async_copy(delta.at[...], dg.at[zl, c], r_dl.at[zl, c]).start()

    pick = lax.broadcasted_iota(jnp.int32, (H, 128), 0) == zl
    fin[0:1, :] = jnp.sum(jnp.where(pick, lse, 0.0), axis=0, keepdims=True)
    fin[1:2, :] = jnp.sum(jnp.where(pick, kl, 0.0), axis=0, keepdims=True)
    fi_copy = rc(fin.at[...], fin_in.at[...], s_fi, r_fi, partner)
    fi_copy.start()

    gt[...] = jnp.zeros_like(gt)
    pltpu.make_async_copy(hidt.at[pc], hidt.at[pc], r_ht).wait()

    def consume(kk):
        cols = pl.ds(pl.multiple_of(kk * cs, cs), cs)
        for h in range(2):
            gt[h] += lax.dot_general(
                head[:, cols], dg[kk, h], (((1,), (1,)), ((), ())), preferred_element_type=jnp.float32
            )
        res[...] = jnp.dot(hidt[0], dg[kk, 0], preferred_element_type=jnp.float32) + jnp.dot(
            hidt[1], dg[kk, 1], preferred_element_type=jnp.float32
        )
        ghead_out[:, cols] = res[pl.ds(pl.multiple_of(off, 64), db), :].astype(jnp.bfloat16)

    def dl_arrived(kk, part):
        pltpu.make_async_copy(dg.at[kk, part], dg.at[kk, part], r_dl.at[kk, part]).wait()

    def df_copy(kk, part, direction):
        to = lax.rem(z + 1, Z) if direction == 0 else lax.rem(z + Z - 1, Z)
        view = dg.at[kk, part]
        return rc(view, view, s_df.at[kk, part], r_dl.at[kk, part], dev(x, y, c, to))

    for s in range(1, Z // 2 + 1):
        for part in range(2):
            for direction in range(2):
                if s <= hops[part][direction]:
                    zs = lax.rem(z - s + Z, Z) if direction == 0 else lax.rem(z + s, Z)
                    kk = lax.rem(zs, H)

                    @pl.when(lax.div(zs, H) == c)
                    def _():
                        dl_arrived(kk, part)
                        if s < hops[part][direction]:
                            df_copy(kk, part, direction).start()

    @pl.when(zh == c)
    def _():
        dl_arrived(zl, 0)
        dl_arrived(zl, 1)

    @pl.loop(0, H)
    def _(kk):
        consume(kk)

    gc_copy = rc(gt.at[pc], gc.at[...], s_gc, r_gc, partner)
    gc_copy.start()
    gc_copy.wait()
    gsum[...] = gt[c] + gc[...]

    def gx_copy(o):
        xd = lax.rem(x + o, X)
        lanes = pl.ds(pl.multiple_of(xd * tb, tb), tb)
        return rc(gsum.at[:, lanes], gx.at[X - o], s_gx.at[o], r_gx.at[X - o], to_x(xd))

    for o in range(1, X):
        gx_copy(o).start()
    acc = gsum[:, pl.ds(pl.multiple_of(x * tb, tb), tb)]
    for o in range(1, X):
        gx_copy(o).wait_send()
        pltpu.make_async_copy(gx.at[o], gx.at[o], r_gx.at[o]).wait()
    for o in range(1, X):
        acc = acc + gx[o]
    gx[0] = acc

    sub = db // Y

    def gy_copy(o):
        yd = lax.rem(y + o, Y)
        return rc(
            gx.at[0, pl.ds(pl.multiple_of(yd * sub, sub), sub), :],
            gy.at[Y - o],
            s_gy.at[o],
            r_gy.at[Y - o],
            to_y(yd),
        )

    for o in range(1, Y):
        gy_copy(o).start()
    acc = gx[0, pl.ds(pl.multiple_of(y * sub, sub), sub), :]
    for o in range(1, Y):
        gy_copy(o).wait_send()
        pltpu.make_async_copy(gy.at[o], gy.at[o], r_gy.at[o]).wait()
    for o in range(1, Y):
        acc = acc + gy[o]
    gf[0] = acc

    vt, zt = z * Y + y, c * X + x
    at_home = (vt == v) & (zt == z)
    go_copy = rc(gf.at[0], gf.at[1], s_go, r_go, {"vocab": vt, "tok": zt})
    go_local = pltpu.make_async_copy(gf.at[0], gf.at[1], r_go)

    @pl.when(at_home)
    def _():
        go_local.start()

    @pl.when(jnp.logical_not(at_home))
    def _():
        go_copy.start()

    pltpu.make_async_copy(fin_in.at[...], fin_in.at[...], r_fi).wait()
    mine = jnp.full(fin.shape, jnp.where(zh == c, 1, 0), jnp.int32) > 0
    stat_out[...] = jnp.where(mine, fin[...], fin_in[...])

    for o in order:
        zd, copy = hz_copy(o)

        @pl.when(lax.div(zd, H) == c)
        def _():
            copy.wait_send()

        zd, copy = hd_copy(o)

        @pl.when(lax.div(zd, H) == c)
        def _():
            copy.wait_send()

        zd, copy = te_copy(o)

        @pl.when(lax.div(zd, H) == c)
        def _():
            copy.wait_send()

        zs = lax.rem(z + o, Z)

        @pl.when(lax.div(zs, H) == c)
        def _():
            hf_copy(zs).wait_send()

    @pl.when(zh == c)
    def _():
        own_head.wait_send()

    ht_copy.wait_send()
    dl_copy(0).wait_send()
    if hops[1][1] > 0 and hops[0][1] > 0:
        dl_copy(1).wait_send()
    else:

        @pl.when(c == 1)
        def _():
            dl_copy(1).wait_send()

    @pl.when(zh != c)
    def _():
        dl_local.wait_send()

    fi_copy.wait_send()
    for s in range(1, Z // 2 + 1):
        for part in range(2):
            for direction in range(2):
                if s < hops[part][direction]:
                    zs = lax.rem(z - s + Z, Z) if direction == 0 else lax.rem(z + s, Z)

                    @pl.when(lax.div(zs, H) == c)
                    def _():
                        df_copy(lax.rem(zs, H), part, direction).wait_send()

    @pl.when(jnp.logical_not(at_home))
    def _():
        go_copy.wait_send()

    go_local.wait()
    ghid_out[...] = gf[1]


def per_device(geo, hidden, head, teacher, block_ids, counts):
    X, Y, Z, blk = geo
    H = Z // 2
    tb, d = hidden.shape
    db, cb = head.shape
    cs, th = cb // H, tb * H
    win = -(-db // 128) * 128
    sub = db // Y
    f32, bf16 = jnp.float32, jnp.bfloat16
    dma = pltpu.SemaphoreType.DMA
    half = max(X, Y) // 2
    scratch = [
        pltpu.VMEM((tb, cb), bf16),
        pltpu.VMEM((H, tb, d), bf16),
        pltpu.VMEM((Z, db, cs), bf16),
        pltpu.VMEM((H, tb, cs), bf16),
        pltpu.VMEM((th, cs), f32),
        pltpu.VMEM((4 * H, 128), f32),
        pltpu.VMEM((3, max(X, Y, Z), 4 * H, 128), f32),
        pltpu.VMEM((th, cs), bf16),
        pltpu.VMEM((H, 2, th, cs), bf16),
        pltpu.VMEM((2, win, th), bf16),
        pltpu.VMEM((win, cs), f32),
        pltpu.VMEM((2, db, th), f32),
        pltpu.VMEM((db, th), f32),
        pltpu.VMEM((X, db, tb), f32),
        pltpu.VMEM((Y, sub, tb), f32),
        pltpu.VMEM((2, sub, tb), f32),
        pltpu.VMEM((db, th), f32),
        pltpu.VMEM((8, 128), f32),
        pltpu.VMEM((8, 128), f32),
        dma((Z,)), dma((H,)),
        dma((2, 2, 2, half)), dma((2, 2, 2, half)),
        dma((Z,)), dma((H,)), dma((Z,)),
        dma((Z,)), dma((H,)),
        dma((3, max(X, Y, Z))), dma((3, max(X, Y, Z))),
        dma((3,)), dma((H, 2)), dma((H, 2)),
        dma, dma,
        dma, dma,
        dma((X,)), dma((X,)),
        dma((Y,)), dma((Y,)),
        dma, dma,
        dma, dma,
    ]
    vm = pl.BlockSpec(memory_space=pltpu.VMEM)
    sm = pl.BlockSpec(memory_space=pltpu.SMEM)
    ghead, ghid, stats = pl.pallas_call(
        functools.partial(kernel_body, geo),
        out_shape=(
            jax.ShapeDtypeStruct((db, cb), bf16),
            jax.ShapeDtypeStruct((sub, tb), f32),
            jax.ShapeDtypeStruct((8, 128), f32),
        ),
        in_specs=[vm, vm, vm, sm, sm],
        out_specs=(vm, vm, vm),
        scratch_shapes=scratch,
        compiler_params=pltpu.CompilerParams(has_side_effects=True, vmem_limit_bytes=60 * 2**20),
    )(hidden, head, teacher, block_ids, counts)
    return stats[0], stats[1], ghid.T, ghead


def solution(mesh, ring_y=RING_Y, blk=BLK):
    vocab, tok = mesh.shape["vocab"], mesh.shape["tok"]
    geo = (vocab // (2 * ring_y), ring_y, tok, blk)
    placed = (P("tok", None), P("tok", "vocab"), P("tok", "vocab"), P("tok", None), P("tok"))
    return jax.shard_map(
        functools.partial(per_device, geo),
        mesh=mesh,
        in_specs=placed,
        out_specs=(P("tok"), P("tok"), P("tok", "vocab"), P("tok", "vocab")),
        check_vma=False,
    )
```

```python
import functools

import jax
import jax.numpy as jnp
from jax import lax
from jax.experimental import pallas as pl
from jax.experimental.pallas import tpu as pltpu
from jax.sharding import PartitionSpec as P

BLK = 512
RING_Y = 8

MESH = pl.DeviceIdType.MESH
loss_scale = 1024.0


def ring_hops(n, parts):
    if parts == 1:
        return [(n // 2, (n - 1) // 2)]
    return [(n // 2, (n - 1) // 2), ((n - 1) // 2, n // 2)]


def kernel_body(
    geo,
    hidden, head_in, teacher_in, ids, counts,
    ghead_out, ghid_out, stat_out,
    head, teacher, kept, hid, headt, teach, logits, masses, mass_in, terms, term_in, stat, stat_in, delta, dg, hidt, res, ghead, gt, gc, gx, gy, gf, gsum, fin, fin_in,
    s_in, s_gh, s_hz, r_hz, s_ga, r_ga, r_gb, s_hd, s_hf, r_hd, s_te, r_te, s_ms, r_ms, s_tm, r_tm, s_tz, s_st, r_st, s_dl, s_df, r_dl, s_ht, r_ht,
    s_gc, r_gc, s_gx, r_gx, s_gy, r_gy, s_go, r_go, s_fi, r_fi,
):
    X, Y, Z, blk = geo
    H = Z // 2
    tb, d = hidden.shape
    db, cb = head_in.shape
    cs = cb // H
    th = tb * H
    v = lax.axis_index("vocab")
    z = lax.axis_index("tok")
    c = lax.rem(v, 2)
    y = lax.rem(lax.div(v, 2), Y)
    x = lax.div(v, 2 * Y)
    zh, zl = lax.div(z, H), lax.rem(z, H)
    pc = 1 - c

    def dev(xx, yy, cc, zz):
        return {"vocab": (xx * Y + yy) * 2 + cc, "tok": zz}

    def rc(src, dst, ssem, rsem, device):
        return pltpu.make_async_remote_copy(
            src_ref=src, dst_ref=dst, send_sem=ssem, recv_sem=rsem, device_id=device, device_id_type=MESH
        )

    partner = dev(x, y, pc, z)

    def rows_of(yy, zz):
        return lax.rem(yy + Y // 4 + (Y // 2) * lax.rem(zz, 2), Y)

    def tokens_of(xx, cc, zz):
        same = lax.rem(cc + lax.div(zz, H) + 1, 2)
        return lax.rem(lax.rem(zz, H) + xx + X - lax.div(zz, 2) + (H // 2) * same, H)

    vt, zt = z * Y + rows_of(y, z), c * H + tokens_of(x, c, z)
    at_home = (vt == v) & (zt == z)
    zs_home, cs_home = lax.div(v, Y), zh
    same_home = lax.rem(cs_home + lax.div(zs_home, H) + 1, 2)
    ys_home = lax.rem(lax.rem(v, Y) + 2 * Y - Y // 4 - (Y // 2) * lax.rem(zs_home, 2), Y)
    xs_home = lax.rem(zl + 2 * H - lax.rem(zs_home, H) - (H // 2) * same_home + lax.div(zs_home, 2), X)
    vs = (xs_home * Y + ys_home) * 2 + cs_home

    barrier = pltpu.get_barrier_semaphore()

    def greet(device):
        pl.semaphore_signal(barrier, inc=1, device_id=device, device_id_type=MESH)

    greet(partner)
    for o in range(1, Z):
        for cc in range(2):
            greet(dev(x, y, cc, lax.rem(z + o, Z)))
    for o in range(1, X):
        greet(dev(lax.rem(x + o, X), y, c, z))
    for o in range(1, Y):
        greet(dev(x, lax.rem(y + o, Y), c, z))

    @pl.when(jnp.logical_not(at_home))
    def _():
        greet({"vocab": vt, "tok": zt})
        greet({"vocab": vs, "tok": zs_home})

    head_copy = pltpu.make_async_copy(head_in, head, s_in.at[0])
    teacher_copy = pltpu.make_async_copy(teacher_in, teacher, s_in.at[1])
    teacher_copy.start()
    head_copy.start()

    near = 1 + 2 * (Z - 1) + (X - 1) + (Y - 1)
    pl.semaphore_wait(barrier, jnp.where(at_home, near, near + 2))

    order = sorted(range(1, Z), key=lambda o: min(o, Z - o))

    pr, plan = tb // Y, d // X
    row0 = pl.multiple_of(y * pr, pr)
    lane0 = pl.multiple_of(x * plan, plan)
    piece = hidden.at[pl.ds(row0, pr), pl.ds(lane0, plan)]
    piece_to = hid.at[zl, pl.ds(row0, pr), pl.ds(lane0, plan)]

    def hz_copy(o):
        zd = lax.rem(z + o, Z)
        return zd, rc(piece, piece_to, s_hz.at[o], r_hz.at[zl], dev(x, y, zh, zd))

    for o in order:
        zd, copy = hz_copy(o)

        @pl.when(lax.div(zd, H) == c)
        def _():
            copy.start()

    @pl.when(zh == c)
    def _():
        pltpu.make_async_copy(piece, piece_to, r_hz.at[zl]).start()

    def hd_copy(o):
        zd = lax.rem(z + o, Z)
        cols = pl.ds(pl.multiple_of(lax.rem(zd, H) * cs, cs), cs)
        return zd, rc(head_in.at[:, cols], headt.at[z], s_hd.at[o], r_hd.at[z], dev(x, y, zh, zd))

    for o in order:
        zd, copy = hd_copy(o)

        @pl.when(lax.div(zd, H) == c)
        def _():
            copy.start()

    own_cols = pl.ds(pl.multiple_of(zl * cs, cs), cs)

    own_head = rc(head_in.at[:, own_cols], headt.at[z], s_hd.at[0], r_hd.at[z], partner)

    @pl.when(zh == c)
    def _():
        pltpu.make_async_copy(head_in.at[:, own_cols], headt.at[z], r_hd.at[z]).start()
        own_head.start()

    slots = ids.shape[1]
    teacher_copy.wait()
    local_mass = jnp.zeros((tb, 1), jnp.float32)
    for k in range(cb // blk):
        block = v * (cb // blk) + k
        hit = jnp.int32(0)
        for s in range(slots):
            hit = hit | jnp.where((ids[0, s] == block) & (s < counts[0]), 1, 0)
        part = teacher[:, k * blk : (k + 1) * blk]
        keep = jnp.full(part.shape, hit, jnp.int32) > 0
        part = jnp.where(keep, part.astype(jnp.float32), 0.0)
        kept[:, k * blk : (k + 1) * blk] = part.astype(jnp.bfloat16)
        local_mass = local_mass + jnp.sum(part, axis=1, keepdims=True)

    def te_copy(o):
        zd = lax.rem(z + o, Z)
        cols = pl.ds(pl.multiple_of(lax.rem(zd, H) * cs, cs), cs)
        return zd, rc(kept.at[:, cols], teach.at[zl], s_te.at[o], r_te.at[zl], dev(x, y, zh, zd))

    for o in order:
        zd, copy = te_copy(o)

        @pl.when(lax.div(zd, H) == c)
        def _():
            copy.start()

    @pl.when(zh == c)
    def _():
        pltpu.make_async_copy(kept.at[:, own_cols], teach.at[zl], r_te.at[zl]).start()

    masses[...] = jnp.broadcast_to(local_mass, (tb, 128)).T[0:8, :]

    def share(buffer, inbox, ssem, rsem, n, me, to):
        def start():
            for o in range(1, n):
                rc(buffer, inbox.at[n - o], ssem, rsem, to(lax.rem(me + o, n))).start()

        def arrive():
            if n > 1:
                all_in = inbox.at[pl.ds(1, n - 1)]
                pltpu.make_async_copy(all_in, all_in, ssem).wait()
                pltpu.make_async_copy(all_in, all_in, rsem).wait()

        return start, arrive

    def to_x(i):
        return dev(i, y, c, z)

    def to_y(i):
        return dev(x, i, c, z)

    def summed(buffer, inbox, n):
        total = buffer[...]
        for o in range(1, n):
            total = total + inbox[o]
        buffer[...] = total

    mass_c = rc(masses.at[...], mass_in.at[0, 0], s_ms.at[0], r_ms.at[0], partner)
    mass_x = share(masses.at[...], mass_in.at[1], s_ms.at[1], r_ms.at[1], X, x, to_x)
    mass_y = share(masses.at[...], mass_in.at[2], s_ms.at[2], r_ms.at[2], Y, y, to_y)
    mass_c.start()
    mass_c.wait()
    masses[...] = masses[...] + mass_in[0, 0]
    mass_x[0]()

    for k in range(H):
        pltpu.make_async_copy(piece, hid.at[k, pl.ds(row0, pr), pl.ds(lane0, plan)], r_hz.at[k]).wait()

    def gather(g, first, second, block):
        (n1, me1, to1), (n2, me2, to2) = first, second
        hops1 = ring_hops(n1, 1)[0]

        def along(n, me, direction, s, to):
            source = lax.rem(me - (s - 1) + n, n) if direction == 0 else lax.rem(me + (s - 1), n)
            target = lax.rem(me + 1, n) if direction == 0 else lax.rem(me + n - 1, n)
            return source, to(target)

        def came(n, me, direction, s):
            return lax.rem(me - s + n, n) if direction == 0 else lax.rem(me + s, n)

        def send1(direction, s):
            source, device = along(n1, me1, direction, s, to1)
            view = block(source, me2)
            rc(view, view, s_ga.at[g, 0], r_ga.at[g, direction, s - 1], device).start()

        def wait1(direction, s):
            view = block(came(n1, me1, direction, s), me2)
            pltpu.make_async_copy(view, view, r_ga.at[g, direction, s - 1]).wait()

        def hops2(q):
            right, left = ring_hops(n2, 1)[0]
            return (right, left) if q % 2 == 0 else (left, right)

        def send2(q, direction, s):
            source, device = along(n2, me2, direction, s, to2)
            view = block(lax.rem(me1 + q, n1), source)
            rc(view, view, s_ga.at[g, 1], r_gb.at[g, (2 * q + direction) * (n2 // 2) + s - 1], device).start()

        progress = {}

        def begin2(q):
            progress[q] = 1
            for direction in range(2):
                if hops2(q)[direction] >= 1:
                    send2(q, direction, 1)

        def advance2(q):
            s = progress[q]
            progress[q] += 1
            for direction in range(2):
                if s <= hops2(q)[direction]:
                    view = block(lax.rem(me1 + q, n1), came(n2, me2, direction, s))
                    pltpu.make_async_copy(view, view, r_gb.at[g, (2 * q + direction) * (n2 // 2) + s - 1]).wait()
                    if s < hops2(q)[direction]:
                        send2(q, direction, s + 1)

        for direction in range(2):
            if hops1[direction] >= 1:
                send1(direction, 1)
        begin2(0)
        yield
        for s in range(1, n1 // 2 + 1):
            earlier = list(progress)
            for direction in range(2):
                if s <= hops1[direction]:
                    wait1(direction, s)
                    if s < hops1[direction]:
                        send1(direction, s + 1)
                    begin2(n1 - s if direction == 0 else s)
            yield
            for q in earlier:
                if progress[q] <= n2 // 2:
                    advance2(q)
                    yield
        while any(at <= n2 // 2 for at in progress.values()):
            for q in list(progress):
                if progress[q] <= n2 // 2:
                    advance2(q)
                    yield
    def rows_at(i):
        return pl.ds(pl.multiple_of(i * pr, pr), pr)

    def lanes_at(i):
        return pl.ds(pl.multiple_of(i * plan, plan), plan)

    def hf_copy(zs):
        return rc(headt.at[zs], headt.at[zs], s_hf.at[lax.rem(zs, H)], r_hd.at[zs], partner)

    def head_arrived(zs):
        pltpu.make_async_copy(headt.at[zs], headt.at[zs], r_hd.at[zs]).wait()

    def head_onward(o):
        zs = lax.rem(z + o, Z)

        @pl.when(lax.div(zs, H) == c)
        def _():
            head_arrived(zs)
            hf_copy(zs).start()

    early = Z // 4
    split = H if H == 1 else H // 2
    x_first = gather(
        0, (X, x, to_x), (Y, y, to_y), lambda i, j: hid.at[pl.ds(0, split), rows_at(j), lanes_at(i)]
    )
    y_first = gather(
        1, (Y, y, to_y), (X, x, to_x), lambda i, j: hid.at[pl.ds(split, H - split), rows_at(i), lanes_at(j)]
    )
    todo = [x_first] if split == H else [x_first, y_first]
    turn = 0
    while todo:
        todo = [walk for walk in todo if next(walk, todo) is not todo]
        turn += 1
        if turn == 3:
            mass_x[1]()
            summed(masses, mass_in.at[1], X)
            mass_y[0]()
        if turn == 10 and early >= 1:
            head_onward(1)
            head_onward(Z - 1)
    if turn < 3:
        mass_x[1]()
        summed(masses, mass_in.at[1], X)
        mass_y[0]()
    if turn < 10 and early >= 1:
        head_onward(1)
        head_onward(Z - 1)
    for o in range(2, early + 1):
        head_onward(o)
        head_onward(Z - o)

    mass_y[1]()
    summed(masses, mass_in.at[2], Y)

    win = hidt.shape[1]
    win0 = lax.div(z * db, 128) * 128
    off = z * db - win0
    for k in range(H):
        block = hid[k, :, pl.ds(pl.multiple_of(win0, 128), win)]
        hidt[c, :, k * tb : (k + 1) * tb] = block.T
    ht_copy = rc(hidt.at[c], hidt.at[c], s_ht, r_ht, partner)
    ht_copy.start()

    logits[...] = jnp.zeros_like(logits)
    kd = 2 * db
    for step in [0] + [q * sign for q in range(1, H // 2 + 1) for sign in (1, -1)][: H - 1]:
        p = lax.rem(lax.div(z, 2) + step + H, H)
        for zs in (2 * p, 2 * p + 1):

            away = lax.rem(zs - z + Z, Z)
            passed = (away != 0) & ((away <= early) | (away >= Z - early)) & (lax.div(zs, H) == c)
            onward = (away > early) & (away < Z - early) & (lax.div(zs, H) == c)

            @pl.when(jnp.logical_not(passed))
            def _():
                head_arrived(zs)

            @pl.when(onward)
            def _():
                hf_copy(zs).start()

        lhs = hid[:, :, pl.ds(pl.multiple_of(p * kd, 128), kd)].reshape(th, kd)
        rhs = headt[pl.ds(2 * p, 2)].reshape(kd, cs)
        logits[...] += jnp.dot(lhs, rhs, preferred_element_type=jnp.float32)

    lane = lax.broadcasted_iota(jnp.int32, (tb, 128), 1)

    for k in range(H):
        lk = logits[k * tb : (k + 1) * tb, :]
        top = jnp.max(lk, axis=1, keepdims=True)
        total = jnp.sum(jnp.exp(lk - top), axis=1, keepdims=True)
        table = jnp.where(lane == 0, top, total).T
        stat[k : k + 1, :] = table[0:1, :]
        stat[H + k : H + k + 1, :] = table[1:2, :]
    stat[2 * H : 2 * H + 1, :] = masses[0:1, :]

    def exchange(stage, n, me, to):
        start, arrive = share(stat.at[...], stat_in.at[stage], s_st.at[stage], r_st.at[stage], n, me, to)
        start()
        arrive()
        blocks = [stat[...]] + [stat_in[stage, o] for o in range(1, n)]
        top = functools.reduce(jnp.maximum, [b[0:H] for b in blocks])
        total = functools.reduce(jnp.add, [b[H : 2 * H] * jnp.exp(b[0:H] - top) for b in blocks])
        stat[0:H, :] = top
        stat[H : 2 * H, :] = total

    exchange(0, X, x, to_x)
    exchange(1, Y, y, to_y)
    stat_in[2, 0] = stat[...]
    exchange(2, Z, z, lambda i: dev(x, y, c, i))

    for k in range(H):
        pltpu.make_async_copy(teach.at[k], teach.at[k], r_te.at[k]).wait()

    hops = ring_hops(Z, 2)
    nsub = dg.shape[2]
    tsub = th // nsub

    def dl_copy(direction, i):
        to = lax.rem(z + 1, Z) if direction == 0 else lax.rem(z + Z - 1, Z)
        return rc(
            delta.at[pl.ds(i * tsub, tsub)],
            dg.at[zl, c, i],
            s_dl.at[direction, i],
            r_dl.at[zl, c, i],
            dev(x, y, zh, to),
        )

    def dl_local(i):
        return rc(delta.at[pl.ds(i * tsub, tsub)], dg.at[zl, c, i], s_dl.at[2, i], r_dl.at[zl, c, i], partner)

    both_ways = min(hops[0] + hops[1]) > 0

    def send_delta(i):
        dl_copy(0, i).start()
        if both_ways:
            dl_copy(1, i).start()
        else:

            @pl.when(c == 1)
            def _():
                dl_copy(1, i).start()

        @pl.when(zh != c)
        def _():
            dl_local(i).start()

        @pl.when(zh == c)
        def _():
            pltpu.make_async_copy(delta.at[pl.ds(i * tsub, tsub)], dg.at[zl, c, i], r_dl.at[zl, c, i]).start()

    final = stat[...]
    lse = final[0:H] + jnp.log(final[H : 2 * H])
    mass = jnp.concatenate(
        [stat_in[2, lax.rem(c * H + k + Z - z, Z), 2 * H : 2 * H + 1, :] for k in range(H)], axis=0
    )
    scale = loss_scale / mass
    rows = jnp.concatenate([lse, scale, jnp.zeros((128 - 2 * H, 128), jnp.float32)], axis=0).T

    for k in range(H):
        lk = logits[k * tb : (k + 1) * tb, :]
        tk = teach[k].astype(jnp.float32)
        student = jnp.exp(lk - rows[:, k : k + 1])
        delta[k * tb : (k + 1) * tb, :] = (loss_scale * student - tk * rows[:, H + k : H + k + 1]).astype(
            jnp.bfloat16
        )
        if (k + 1) % (H // nsub) == 0:
            send_delta((k + 1) // (H // nsub) - 1)

    for k in range(H):
        lk = logits[k * tb : (k + 1) * tb, :]
        tk = teach[k].astype(jnp.float32)
        live = tk > 0.0
        term = jnp.where(live, tk * (jnp.log(jnp.where(live, tk, 1.0)) - lk), 0.0)
        table = jnp.broadcast_to(jnp.sum(term, axis=1, keepdims=True), (tb, 128)).T
        terms[k : k + 1, :] = table[0:1, :]
    term_x = share(terms.at[...], term_in.at[0], s_tm.at[0], r_tm.at[0], X, x, to_x)
    term_y = share(terms.at[...], term_in.at[1], s_tm.at[1], r_tm.at[1], Y, y, to_y)
    term_x[0]()

    def term_z(o):
        zd = lax.rem(z + o, Z)
        return zd, rc(terms.at[...], term_in.at[2, Z - o], s_tz.at[o], r_tm.at[2], dev(x, y, c, zd))

    def terms_to_y():
        term_x[1]()
        summed(terms, term_in.at[0], X)
        term_y[0]()

    def terms_to_z():
        term_y[1]()
        summed(terms, term_in.at[1], Y)
        for o in order:
            zd, copy = term_z(o)

            @pl.when(lax.div(zd, H) == c)
            def _():
                copy.start()

    def finish_terms():
        for o in order:
            zd, copy = term_z(o)

            @pl.when(lax.div(zd, H) == c)
            def _():
                copy.wait_send()

        @pl.when(zh == c)
        def _():
            all_in = term_in.at[2, pl.ds(1, Z - 1)]
            pltpu.make_async_copy(all_in, all_in, r_tm.at[2]).wait()
            total = terms[0:H, :]
            for o in range(1, Z):
                total = total + term_in[2, o, 0:H, :]
            kl = total / mass - jnp.log(mass) + lse
            pick = lax.broadcasted_iota(jnp.int32, (H, 128), 0) == zl
            fin[0:1, :] = jnp.sum(jnp.where(pick, lse, 0.0), axis=0, keepdims=True)
            fin[1:2, :] = jnp.sum(jnp.where(pick, kl, 0.0), axis=0, keepdims=True)
            fi_copy.start()

    fi_copy = rc(fin.at[...], fin_in.at[...], s_fi, r_fi, partner)

    head_copy.wait()
    gt[...] = jnp.zeros_like(gt)
    pltpu.make_async_copy(hidt.at[pc], hidt.at[pc], r_ht).wait()

    def to_gt(kk):
        cols = pl.ds(pl.multiple_of(kk * cs, cs), cs)
        for h in range(2):
            gt[h] += lax.dot_general(
                head[:, cols], dg[kk, h].reshape(th, cs), (((1,), (1,)), ((), ())), preferred_element_type=jnp.float32
            )

    def to_ghead(kk):
        cols = pl.ds(pl.multiple_of(kk * cs, cs), cs)
        res[...] = jnp.dot(hidt[0], dg[kk, 0].reshape(th, cs), preferred_element_type=jnp.float32) + jnp.dot(
            hidt[1], dg[kk, 1].reshape(th, cs), preferred_element_type=jnp.float32
        )
        ghead[:, cols] = res[pl.ds(pl.multiple_of(off, 64), db), :].astype(jnp.bfloat16)

    def ghead_copy(kk):
        cols = pl.ds(pl.multiple_of(kk * cs, cs), cs)
        return pltpu.make_async_copy(ghead.at[:, cols], ghead_out.at[:, cols], s_gh.at[kk])

    def dl_arrived(kk, part, i):
        pltpu.make_async_copy(dg.at[kk, part, i], dg.at[kk, part, i], r_dl.at[kk, part, i]).wait()

    def df_copy(kk, part, i, direction):
        to = lax.rem(z + 1, Z) if direction == 0 else lax.rem(z + Z - 1, Z)
        view = dg.at[kk, part, i]
        return rc(view, view, s_df.at[kk, part, i], r_dl.at[kk, part, i], dev(x, y, c, to))

    def hop_source(direction, s):
        return lax.rem(z - s + Z, Z) if direction == 0 else lax.rem(z + s, Z)

    for s in range(0, Z // 2 + 1):
        for i in range(nsub if s else 0):
            for part in range(2):
                for direction in range(2):
                    if s <= hops[part][direction]:
                        zs = hop_source(direction, s)
                        kk = lax.rem(zs, H)

                        @pl.when(lax.div(zs, H) == c)
                        def _():
                            dl_arrived(kk, part, i)
                            if s < hops[part][direction]:
                                df_copy(kk, part, i, direction).start()

        if s == 0:

            @pl.when(zh == c)
            def _():
                for part in range(2):
                    for i in range(nsub):
                        dl_arrived(zl, part, i)
                to_gt(zl)
        else:

            @pl.loop(0, 1 if 2 * s == Z else 2)
            def _(i):
                zs = lax.rem(z + Z - s + 2 * s * i, Z)

                @pl.when(lax.div(zs, H) == c)
                def _():
                    to_gt(lax.rem(zs, H))

        if s == 1:
            terms_to_y()
        if s == min(2, Z // 2):
            terms_to_z()

    nd = gx.shape[0]
    rows = db // nd
    sub = db // Y
    x_order = sorted(range(X), key=lambda o: -min(o, X - o))

    def gc_copy(dh, o):
        block = tokens_of(lax.rem(x + o, X), pc, z)
        lanes = pl.ds(pl.multiple_of(block * tb, tb), tb)
        return rc(
            gt.at[pc, pl.ds(dh * rows, rows), lanes], gc.at[dh, o], s_gc, r_gc.at[dh, o], partner
        )

    def gx_copy(dh, o):
        return rc(gsum.at[dh, o], gx.at[dh, X - o], s_gx, r_gx.at[dh], to_x(lax.rem(x + o, X)))

    for dh in range(nd):
        for o in x_order:
            gc_copy(dh, o).start()
    for dh in range(nd):
        for o in x_order:
            block = tokens_of(lax.rem(x + o, X), c, z)
            lanes = pl.ds(pl.multiple_of(block * tb, tb), tb)
            pltpu.make_async_copy(gc.at[dh, o], gc.at[dh, o], r_gc.at[dh, o]).wait()
            gsum[dh, o] = gt[c, dh * rows : (dh + 1) * rows, lanes] + gc[dh, o]
            if o:
                gx_copy(dh, o).start()

    @pl.loop(0, H)
    def _(kk):
        to_ghead(kk)
        ghead_copy(kk).start()

    finish_terms()

    def gy_copy(o):
        yd = lax.rem(y + o, Y)
        i = rows_of(yd, z)
        return i, rc(
            gx.at[lax.div(i * nd, Y), 0, pl.ds(pl.multiple_of(lax.rem(i, Y // nd) * sub, sub), sub), :],
            gy.at[Y - o],
            s_gy,
            r_gy,
            to_y(yd),
        )

    y_order = sorted(range(1, Y), key=lambda o: -min(o, Y - o))
    for dh in range(nd):
        acc = gsum[dh, 0]
        if X > 1:
            all_in = gx.at[dh, pl.ds(1, X - 1)]
            pltpu.make_async_copy(all_in, all_in, r_gx.at[dh]).wait()
        for o in range(1, X):
            acc = acc + gx[dh, o]
        gx[dh, 0] = acc
        for o in y_order:
            i, copy = gy_copy(o)

            @pl.when(lax.div(i * nd, Y) == dh)
            def _():
                copy.start()

    mine = rows_of(y, z)
    acc = gx[lax.div(mine * nd, Y), 0, pl.ds(pl.multiple_of(lax.rem(mine, Y // nd) * sub, sub), sub), :]
    if Y > 1:
        all_in = gy.at[pl.ds(1, Y - 1)]
        pltpu.make_async_copy(all_in, all_in, r_gy).wait()
    for o in range(1, Y):
        acc = acc + gy[o]
    gf[0] = acc

    go_copy = rc(gf.at[0], gf.at[1], s_go, r_go, {"vocab": vt, "tok": zt})
    go_local = pltpu.make_async_copy(gf.at[0], gf.at[1], r_go)

    @pl.when(at_home)
    def _():
        go_local.start()

    @pl.when(jnp.logical_not(at_home))
    def _():
        go_copy.start()

    @pl.when(zh == c)
    def _():
        fi_copy.wait_send()
        stat_out[...] = fin[...]

    @pl.when(zh != c)
    def _():
        pltpu.make_async_copy(fin_in.at[...], fin_in.at[...], r_fi).wait()
        stat_out[...] = fin_in[...]

    pltpu.make_async_copy(gc.at[...], gc.at[...], s_gc).wait()
    if X > 1:
        all_out = gx.at[:, pl.ds(1, X - 1)]
        pltpu.make_async_copy(all_out, all_out, s_gx).wait()
    if Y > 1:
        all_out = gy.at[pl.ds(1, Y - 1)]
        pltpu.make_async_copy(all_out, all_out, s_gy).wait()

    def drain(k0, kn, nrows, nlanes, sem):
        if min(kn, nrows, nlanes) > 0:
            view = hid.at[pl.ds(k0, kn), pl.ds(0, nrows), pl.ds(0, nlanes)]
            pltpu.make_async_copy(view, view, sem).wait()

    drain(0, split, pr, (X - 1) * plan, s_ga.at[0, 0])
    drain(0, split, (Y - 1) * pr, d, s_ga.at[0, 1])
    drain(split, H - split, (Y - 1) * pr, plan, s_ga.at[1, 0])
    drain(split, H - split, tb, (X - 1) * plan, s_ga.at[1, 1])
    for o in order:
        zd, copy = hz_copy(o)

        @pl.when(lax.div(zd, H) == c)
        def _():
            copy.wait_send()

        zd, copy = hd_copy(o)

        @pl.when(lax.div(zd, H) == c)
        def _():
            copy.wait_send()

        zd, copy = te_copy(o)

        @pl.when(lax.div(zd, H) == c)
        def _():
            copy.wait_send()

        zs = lax.rem(z + o, Z)

        @pl.when(lax.div(zs, H) == c)
        def _():
            hf_copy(zs).wait_send()

    @pl.when(zh == c)
    def _():
        own_head.wait_send()

    ht_copy.wait_send()
    for i in range(nsub):
        dl_copy(0, i).wait_send()
        if both_ways:
            dl_copy(1, i).wait_send()
        else:

            @pl.when(c == 1)
            def _():
                dl_copy(1, i).wait_send()

        @pl.when(zh != c)
        def _():
            dl_local(i).wait_send()

        for s in range(1, Z // 2 + 1):
            for part in range(2):
                for direction in range(2):
                    if s < hops[part][direction]:
                        zs = hop_source(direction, s)

                        @pl.when(lax.div(zs, H) == c)
                        def _():
                            df_copy(lax.rem(zs, H), part, i, direction).wait_send()

    @pl.when(jnp.logical_not(at_home))
    def _():
        go_copy.wait_send()

    for kk in range(H):
        ghead_copy(kk).wait()

    go_local.wait()
    ghid_out[...] = gf[1]


def per_device(geo, hidden, head, teacher, block_ids, counts):
    X, Y, Z, blk = geo
    H = Z // 2
    tb, d = hidden.shape
    db, cb = head.shape
    cs, th = cb // H, tb * H
    win = -(-db // 128) * 128
    sub = db // Y
    f32, bf16 = jnp.float32, jnp.bfloat16
    dma = pltpu.SemaphoreType.DMA
    most = max(X, Y)
    half = max(most // 2, 1)
    nd = 2 if Y % 2 == 0 else 1
    nsub = 2 if H % 2 == 0 else 1
    scratch = [
        pltpu.VMEM((db, cb), bf16),
        pltpu.VMEM((tb, cb), bf16),
        pltpu.VMEM((tb, cb), bf16),
        pltpu.VMEM((H, tb, d), bf16),
        pltpu.VMEM((Z, db, cs), bf16),
        pltpu.VMEM((H, tb, cs), bf16),
        pltpu.VMEM((th, cs), f32),
        pltpu.VMEM((8, 128), f32),
        pltpu.VMEM((3, max(X, Y), 8, 128), f32),
        pltpu.VMEM((8, 128), f32),
        pltpu.VMEM((3, max(X, Y, Z), 8, 128), f32),
        pltpu.VMEM((4 * H, 128), f32),
        pltpu.VMEM((3, max(X, Y, Z), 4 * H, 128), f32),
        pltpu.VMEM((th, cs), bf16),
        pltpu.VMEM((H, 2, nsub, th // nsub, cs), bf16),
        pltpu.VMEM((2, win, th), bf16),
        pltpu.VMEM((win, cs), f32),
        pltpu.VMEM((db, cb), bf16),
        pltpu.VMEM((2, db, th), f32),
        pltpu.VMEM((nd, X, db // nd, tb), f32),
        pltpu.VMEM((nd, X, db // nd, tb), f32),
        pltpu.VMEM((Y, sub, tb), f32),
        pltpu.VMEM((2, sub, tb), f32),
        pltpu.VMEM((nd, X, db // nd, tb), f32),
        pltpu.VMEM((8, 128), f32),
        pltpu.VMEM((8, 128), f32),
        dma((2,)), dma((H,)),
        dma((Z,)), dma((H,)),
        dma((2, 2)), dma((2, 2, half)), dma((2, max(X * Y, 2 * X, 2 * Y))),
        dma((Z,)), dma((H,)), dma((Z,)),
        dma((Z,)), dma((H,)),
        dma((3,)), dma((3,)),
        dma((2,)), dma((3,)), dma((Z,)),
        dma((3,)), dma((3,)),
        dma((3, nsub)), dma((H, 2, nsub)), dma((H, 2, nsub)),
        dma, dma,
        dma, dma((nd, X)),
        dma, dma((nd,)),
        dma, dma,
        dma, dma,
        dma, dma,
    ]
    vm = pl.BlockSpec(memory_space=pltpu.VMEM)
    hbm = pl.BlockSpec(memory_space=pl.ANY)
    sm = pl.BlockSpec(memory_space=pltpu.SMEM)
    ghead, ghid, stats = pl.pallas_call(
        functools.partial(kernel_body, geo),
        out_shape=(
            jax.ShapeDtypeStruct((db, cb), bf16),
            jax.ShapeDtypeStruct((sub, tb), f32),
            jax.ShapeDtypeStruct((8, 128), f32),
        ),
        in_specs=[hbm, hbm, hbm, sm, sm],
        out_specs=(hbm, vm, vm),
        scratch_shapes=scratch,
        compiler_params=pltpu.CompilerParams(has_side_effects=True, collective_id=0, vmem_limit_bytes=60 * 2**20),
    )(hidden, head, teacher, block_ids, counts)

    def place(
        stats_in, ghid_in, ghead_in, lse_to, kl_to, ghid_to, ghead_to, stats_at, ghid_at, ghead_at, in_sem, out_sem
    ):
        moves = [(stats_in, stats_at), (ghid_in, ghid_at)]
        parts = [pl.ds(k * cs, cs) for k in range(H)]
        moves += [(ghead_in.at[:, part], ghead_at.at[:, part]) for part in parts]
        loads = [pltpu.make_async_copy(src, dst, in_sem.at[k]) for k, (src, dst) in enumerate(moves)]
        for load in loads:
            load.start()
        loads[0].wait()
        stores = [
            pltpu.make_async_copy(stats_at.at[pl.ds(0, 1)], lse_to, out_sem.at[0]),
            pltpu.make_async_copy(stats_at.at[pl.ds(1, 1)], kl_to, out_sem.at[1]),
        ]
        stores[0].start()
        stores[1].start()
        loads[1].wait()
        stores.append(pltpu.make_async_copy(ghid_at, ghid_to, out_sem.at[2]))
        stores[2].start()
        for k, part in enumerate(parts):
            loads[2 + k].wait()
            stores.append(pltpu.make_async_copy(ghead_at.at[:, part], ghead_to.at[:, part], out_sem.at[3 + k]))
            stores[3 + k].start()
        for store in stores:
            store.wait()

    lse, kl, ghid, ghead = pl.pallas_call(
        place,
        out_shape=(
            jax.ShapeDtypeStruct((1, tb), f32),
            jax.ShapeDtypeStruct((1, tb), f32),
            jax.ShapeDtypeStruct(ghid.shape, f32),
            jax.ShapeDtypeStruct(ghead.shape, bf16),
        ),
        in_specs=[hbm, hbm, hbm],
        out_specs=(hbm, hbm, hbm, hbm),
        scratch_shapes=[
            pltpu.VMEM((8, 128), f32),
            pltpu.VMEM(ghid.shape, f32),
            pltpu.VMEM(ghead.shape, bf16),
            dma((2 + H,)),
            dma((3 + H,)),
        ],
    )(stats, ghid, ghead)
    return lse.reshape(tb), kl.reshape(tb), ghid.T, ghead


def solution(mesh, ring_y=RING_Y, blk=BLK):
    vocab, tok = mesh.shape["vocab"], mesh.shape["tok"]
    geo = (vocab // (2 * ring_y), ring_y, tok, blk)
    placed = (P("tok", None), P("tok", "vocab"), P("tok", "vocab"), P("tok", None), P("tok"))
    return jax.shard_map(
        functools.partial(per_device, geo),
        mesh=mesh,
        in_specs=placed,
        out_specs=(P("tok"), P("tok"), P("tok", "vocab"), P("tok", "vocab")),
        check_vma=False,
    )
```

```python
import functools

import jax
import jax.numpy as jnp
from jax import lax
from jax.experimental import pallas as pl
from jax.experimental.pallas import tpu as pltpu
from jax.sharding import PartitionSpec as P

BLK = 512
RING_Y = 8

MESH = pl.DeviceIdType.MESH
loss_scale = 1024.0


def ring_hops(n, parts):
    if parts == 1:
        return [(n // 2, (n - 1) // 2)]
    return [(n // 2, (n - 1) // 2), ((n - 1) // 2, n // 2)]


def kernel_body(
    geo,
    hidden, head_in, teacher_in, ids, counts,
    ghead_out, ghid_out, stat_out,
    head, teacher, kept, hid, headt, teach, logits, masses, mass_in, mass_of, terms, term_in, stat, stat_in, delta, dg, hidt, res, ghead, gt, gc, gx, gy, gf, gsum, fin, fin_in,
    s_in, s_gh, s_hz, r_hz, s_ga, r_ga, r_gb, s_hd, s_hf, r_hd, s_te, r_te, s_ms, r_ms, s_mz, r_mz, s_tm, r_tm, s_tz, s_st, r_st, s_dl, s_df, r_dl, s_ht, r_ht,
    s_gc, r_gc, s_gx, r_gx, s_gy, r_gy, s_go, r_go, s_fi, r_fi,
):
    X, Y, Z, blk = geo
    H = Z // 2
    tb, d = hidden.shape
    db, cb = head_in.shape
    cs = cb // H
    th = tb * H
    v = lax.axis_index("vocab")
    z = lax.axis_index("tok")
    c = lax.rem(v, 2)
    y = lax.rem(lax.div(v, 2), Y)
    x = lax.div(v, 2 * Y)
    zh, zl = lax.div(z, H), lax.rem(z, H)
    pc = 1 - c

    def dev(xx, yy, cc, zz):
        return {"vocab": (xx * Y + yy) * 2 + cc, "tok": zz}

    def rc(src, dst, ssem, rsem, device):
        return pltpu.make_async_remote_copy(
            src_ref=src, dst_ref=dst, send_sem=ssem, recv_sem=rsem, device_id=device, device_id_type=MESH
        )

    partner = dev(x, y, pc, z)

    def rows_of(yy, zz):
        return lax.rem(yy + Y // 4 + (Y // 2) * lax.rem(zz, 2), Y)

    def tokens_of(xx, cc, zz):
        same = lax.rem(cc + lax.div(zz, H) + 1, 2)
        return lax.rem(lax.rem(zz, H) + xx + X - lax.div(zz, 2) + (H // 2) * same, H)

    vt, zt = z * Y + rows_of(y, z), c * H + tokens_of(x, c, z)
    at_home = (vt == v) & (zt == z)
    zs_home, cs_home = lax.div(v, Y), zh
    same_home = lax.rem(cs_home + lax.div(zs_home, H) + 1, 2)
    ys_home = lax.rem(lax.rem(v, Y) + 2 * Y - Y // 4 - (Y // 2) * lax.rem(zs_home, 2), Y)
    xs_home = lax.rem(zl + 2 * H - lax.rem(zs_home, H) - (H // 2) * same_home + lax.div(zs_home, 2), X)
    vs = (xs_home * Y + ys_home) * 2 + cs_home

    barrier = pltpu.get_barrier_semaphore()

    def greet(device):
        pl.semaphore_signal(barrier, inc=1, device_id=device, device_id_type=MESH)

    greet(partner)
    for o in range(1, Z):
        for cc in range(2):
            greet(dev(x, y, cc, lax.rem(z + o, Z)))
    for o in range(1, X):
        greet(dev(lax.rem(x + o, X), y, c, z))
    for o in range(1, Y):
        greet(dev(x, lax.rem(y + o, Y), c, z))

    @pl.when(jnp.logical_not(at_home))
    def _():
        greet({"vocab": vt, "tok": zt})
        greet({"vocab": vs, "tok": zs_home})

    head_copy = pltpu.make_async_copy(head_in, head, s_in.at[0])
    teacher_copy = pltpu.make_async_copy(teacher_in, teacher, s_in.at[1])
    teacher_copy.start()
    head_copy.start()

    near = 1 + 2 * (Z - 1) + (X - 1) + (Y - 1)
    pl.semaphore_wait(barrier, jnp.where(at_home, near, near + 2))

    order = sorted(range(1, Z), key=lambda o: min(o, Z - o))

    pr, plan = tb // Y, d // X
    row0 = pl.multiple_of(y * pr, pr)
    lane0 = pl.multiple_of(x * plan, plan)
    piece = hidden.at[pl.ds(row0, pr), pl.ds(lane0, plan)]
    piece_to = hid.at[zl, pl.ds(row0, pr), pl.ds(lane0, plan)]

    def hz_copy(o):
        zd = lax.rem(z + o, Z)
        return zd, rc(piece, piece_to, s_hz.at[lax.rem(zd, H)], r_hz.at[zl], dev(x, y, zh, zd))

    for o in order:
        zd, copy = hz_copy(o)

        @pl.when(lax.div(zd, H) == c)
        def _():
            copy.start()

    @pl.when(zh == c)
    def _():
        pltpu.make_async_copy(piece, piece_to, r_hz.at[zl]).start()

    def hd_copy(o):
        zd = lax.rem(z + o, Z)
        cols = pl.ds(pl.multiple_of(lax.rem(zd, H) * cs, cs), cs)
        return zd, rc(head_in.at[:, cols], headt.at[z], s_hd.at[o], r_hd.at[z], dev(x, y, zh, zd))

    for o in order:
        zd, copy = hd_copy(o)

        @pl.when(lax.div(zd, H) == c)
        def _():
            copy.start()

    own_cols = pl.ds(pl.multiple_of(zl * cs, cs), cs)

    own_head = rc(head_in.at[:, own_cols], headt.at[z], s_hd.at[0], r_hd.at[z], partner)

    @pl.when(zh == c)
    def _():
        pltpu.make_async_copy(head_in.at[:, own_cols], headt.at[z], r_hd.at[z]).start()
        own_head.start()

    slots = ids.shape[1]
    teacher_copy.wait()
    local_mass = jnp.zeros((tb, 1), jnp.float32)
    for k in range(cb // blk):
        block = v * (cb // blk) + k
        hit = jnp.int32(0)
        for s in range(slots):
            hit = hit | jnp.where((ids[0, s] == block) & (s < counts[0]), 1, 0)
        part = teacher[:, k * blk : (k + 1) * blk]
        keep = jnp.full(part.shape, hit, jnp.int32) > 0
        part = jnp.where(keep, part.astype(jnp.float32), 0.0)
        kept[:, k * blk : (k + 1) * blk] = part.astype(jnp.bfloat16)
        local_mass = local_mass + jnp.sum(part, axis=1, keepdims=True)

    def te_copy(o):
        zd = lax.rem(z + o, Z)
        cols = pl.ds(pl.multiple_of(lax.rem(zd, H) * cs, cs), cs)
        return zd, rc(kept.at[:, cols], teach.at[zl], s_te.at[lax.rem(zd, H)], r_te.at[zl], dev(x, y, zh, zd))

    for o in order:
        zd, copy = te_copy(o)

        @pl.when(lax.div(zd, H) == c)
        def _():
            copy.start()

    @pl.when(zh == c)
    def _():
        pltpu.make_async_copy(kept.at[:, own_cols], teach.at[zl], r_te.at[zl]).start()

    masses[...] = jnp.broadcast_to(local_mass, (tb, 128)).T[0:8, :]

    def share(buffer, inbox, ssem, rsem, n, me, to):
        def start():
            for o in range(1, n):
                rc(buffer, inbox.at[n - o], ssem, rsem, to(lax.rem(me + o, n))).start()

        def arrive():
            if n > 1:
                all_in = inbox.at[pl.ds(1, n - 1)]
                pltpu.make_async_copy(all_in, all_in, ssem).wait()
                pltpu.make_async_copy(all_in, all_in, rsem).wait()

        return start, arrive

    def to_x(i):
        return dev(i, y, c, z)

    def to_y(i):
        return dev(x, i, c, z)

    def summed(buffer, inbox, n):
        total = buffer[...]
        for o in range(1, n):
            total = total + inbox[o]
        buffer[...] = total

    mass_c = rc(masses.at[...], mass_in.at[0, 0], s_ms.at[0], r_ms.at[0], partner)
    mass_x = share(masses.at[...], mass_in.at[1], s_ms.at[1], r_ms.at[1], X, x, to_x)
    mass_y = share(masses.at[...], mass_in.at[2], s_ms.at[2], r_ms.at[2], Y, y, to_y)
    mass_c.start()
    mass_c.wait()
    masses[...] = masses[...] + mass_in[0, 0]
    mass_x[0]()

    def gather(g, planes, first, second, block):
        (n1, me1, to1), (n2, me2, to2) = first, second
        hops1 = ring_hops(n1, 1)[0]

        def along(n, me, direction, s, to):
            source = lax.rem(me - (s - 1) + n, n) if direction == 0 else lax.rem(me + (s - 1), n)
            target = lax.rem(me + 1, n) if direction == 0 else lax.rem(me + n - 1, n)
            return source, to(target)

        def came(n, me, direction, s):
            return lax.rem(me - s + n, n) if direction == 0 else lax.rem(me + s, n)

        def send1(direction, s):
            source, device = along(n1, me1, direction, s, to1)
            view = block(source, me2)
            rc(view, view, s_ga.at[g, 0], r_ga.at[g, direction, s - 1], device).start()

        def wait1(direction, s):
            view = block(came(n1, me1, direction, s), me2)
            pltpu.make_async_copy(view, view, r_ga.at[g, direction, s - 1]).wait()

        def hops2(q):
            right, left = ring_hops(n2, 1)[0]
            return (right, left) if q % 2 == 0 else (left, right)

        def send2(q, direction, s):
            source, device = along(n2, me2, direction, s, to2)
            view = block(lax.rem(me1 + q, n1), source)
            rc(view, view, s_ga.at[g, 1], r_gb.at[g, (2 * q + direction) * (n2 // 2) + s - 1], device).start()

        for k in planes:
            pltpu.make_async_copy(piece, hid.at[k, pl.ds(row0, pr), pl.ds(lane0, plan)], r_hz.at[k]).wait()

        progress = {}

        def begin2(q):
            progress[q] = 1
            for direction in range(2):
                if hops2(q)[direction] >= 1:
                    send2(q, direction, 1)

        def advance2(q):
            s = progress[q]
            progress[q] += 1
            for direction in range(2):
                if s <= hops2(q)[direction]:
                    view = block(lax.rem(me1 + q, n1), came(n2, me2, direction, s))
                    pltpu.make_async_copy(view, view, r_gb.at[g, (2 * q + direction) * (n2 // 2) + s - 1]).wait()
                    if s < hops2(q)[direction]:
                        send2(q, direction, s + 1)

        for direction in range(2):
            if hops1[direction] >= 1:
                send1(direction, 1)
        begin2(0)
        yield
        for s in range(1, n1 // 2 + 1):
            earlier = list(progress)
            for direction in range(2):
                if s <= hops1[direction]:
                    wait1(direction, s)
                    if s < hops1[direction]:
                        send1(direction, s + 1)
                    begin2(n1 - s if direction == 0 else s)
            yield
            for q in earlier:
                if progress[q] <= n2 // 2:
                    advance2(q)
                    yield
        while any(at <= n2 // 2 for at in progress.values()):
            for q in list(progress):
                if progress[q] <= n2 // 2:
                    advance2(q)
                    yield
    def rows_at(i):
        return pl.ds(pl.multiple_of(i * pr, pr), pr)

    def lanes_at(i):
        return pl.ds(pl.multiple_of(i * plan, plan), plan)

    def hf_copy(zs):
        return rc(headt.at[zs], headt.at[zs], s_hf.at[lax.rem(zs, H)], r_hd.at[zs], partner)

    def head_arrived(zs):
        pltpu.make_async_copy(headt.at[zs], headt.at[zs], r_hd.at[zs]).wait()

    def head_onward(o):
        zs = lax.rem(z + o, Z)

        @pl.when(lax.div(zs, H) == c)
        def _():
            head_arrived(zs)
            hf_copy(zs).start()

    early = Z // 4
    split = H if H == 1 else H // 2
    x_first = gather(
        0, range(split), (X, x, to_x), (Y, y, to_y), lambda i, j: hid.at[pl.ds(0, split), rows_at(j), lanes_at(i)]
    )
    y_first = gather(
        1, range(split, H), (Y, y, to_y), (X, x, to_x), lambda i, j: hid.at[pl.ds(split, H - split), rows_at(i), lanes_at(j)]
    )
    todo = [x_first] if split == H else [x_first, y_first]
    turn = 0
    while todo:
        todo = [walk for walk in todo if next(walk, todo) is not todo]
        turn += 1
        if turn == 8:
            mass_x[1]()
            summed(masses, mass_in.at[1], X)
            mass_y[0]()
    if turn < 8:
        mass_x[1]()
        summed(masses, mass_in.at[1], X)
        mass_y[0]()
    for o in range(1, early + 1):
        head_onward(o)
        head_onward(Z - o)

    mass_y[1]()
    summed(masses, mass_in.at[2], Y)

    def mass_z(o):
        zd = lax.rem(z + o, Z)
        return zd, rc(masses, mass_of.at[zl], s_mz.at[lax.rem(zd, H)], r_mz.at[zl], dev(x, y, zh, zd))

    for o in order:
        zd, copy = mass_z(o)

        @pl.when(lax.div(zd, H) == c)
        def _():
            copy.start()

    @pl.when(zh == c)
    def _():
        pltpu.make_async_copy(masses, mass_of.at[zl], r_mz.at[zl]).start()

    win = hidt.shape[1]
    win0 = lax.div(z * db, 128) * 128
    off = z * db - win0
    for k in range(H):
        block = hid[k, :, pl.ds(pl.multiple_of(win0, 128), win)]
        hidt[c, :, k * tb : (k + 1) * tb] = block.T
    ht_copy = rc(hidt.at[c], hidt.at[c], s_ht, r_ht, partner)
    ht_copy.start()

    logits[...] = jnp.zeros_like(logits)
    kd = 2 * db
    for step in [0] + [q * sign for q in range(1, H // 2 + 1) for sign in (1, -1)][: H - 1]:
        p = lax.rem(lax.div(z, 2) + step + H, H)
        for zs in (2 * p, 2 * p + 1):

            away = lax.rem(zs - z + Z, Z)
            passed = (away != 0) & ((away <= early) | (away >= Z - early)) & (lax.div(zs, H) == c)
            onward = (away > early) & (away < Z - early) & (lax.div(zs, H) == c)

            @pl.when(jnp.logical_not(passed))
            def _():
                head_arrived(zs)

            @pl.when(onward)
            def _():
                hf_copy(zs).start()

        lhs = hid[:, :, pl.ds(pl.multiple_of(p * kd, 128), kd)].reshape(th, kd)
        rhs = headt[pl.ds(2 * p, 2)].reshape(kd, cs)
        logits[...] += jnp.dot(lhs, rhs, preferred_element_type=jnp.float32)

    lane = lax.broadcasted_iota(jnp.int32, (tb, 128), 1)

    for k in range(H):
        lk = logits[k * tb : (k + 1) * tb, :]
        top = jnp.max(lk, axis=1, keepdims=True)
        total = jnp.sum(jnp.exp(lk - top), axis=1, keepdims=True)
        table = jnp.where(lane == 0, top, total).T
        stat[k : k + 1, :] = table[0:1, :]
        stat[H + k : H + k + 1, :] = table[1:2, :]

    def exchange(stage, n, me, to):
        start, arrive = share(stat.at[...], stat_in.at[stage], s_st.at[stage], r_st.at[stage], n, me, to)
        start()
        arrive()
        blocks = [stat[...]] + [stat_in[stage, o] for o in range(1, n)]
        top = functools.reduce(jnp.maximum, [b[0:H] for b in blocks])
        total = functools.reduce(jnp.add, [b[H : 2 * H] * jnp.exp(b[0:H] - top) for b in blocks])
        stat[0:H, :] = top
        stat[H : 2 * H, :] = total

    exchange(0, X, x, to_x)
    exchange(1, Y, y, to_y)
    exchange(2, Z, z, lambda i: dev(x, y, c, i))

    for k in range(H):
        pltpu.make_async_copy(teach.at[k], teach.at[k], r_te.at[k]).wait()

    hops = ring_hops(Z, 2)
    nsub = dg.shape[2]
    tsub = th // nsub

    def dl_copy(direction, i):
        to = lax.rem(z + 1, Z) if direction == 0 else lax.rem(z + Z - 1, Z)
        return rc(
            delta.at[pl.ds(i * tsub, tsub)],
            dg.at[zl, c, i],
            s_dl.at[direction, i],
            r_dl.at[zl, c, i],
            dev(x, y, zh, to),
        )

    def dl_local(i):
        return rc(delta.at[pl.ds(i * tsub, tsub)], dg.at[zl, c, i], s_dl.at[2, i], r_dl.at[zl, c, i], partner)

    both_ways = min(hops[0] + hops[1]) > 0

    def send_delta(i):
        dl_copy(0, i).start()
        if both_ways:
            dl_copy(1, i).start()
        else:

            @pl.when(c == 1)
            def _():
                dl_copy(1, i).start()

        @pl.when(zh != c)
        def _():
            dl_local(i).start()

        @pl.when(zh == c)
        def _():
            pltpu.make_async_copy(delta.at[pl.ds(i * tsub, tsub)], dg.at[zl, c, i], r_dl.at[zl, c, i]).start()

    final = stat[...]
    lse = final[0:H] + jnp.log(final[H : 2 * H])
    for k in range(H):
        pltpu.make_async_copy(mass_of.at[k], mass_of.at[k], r_mz.at[k]).wait()
    mass = jnp.concatenate([mass_of[k, 0:1, :] for k in range(H)], axis=0)
    scale = loss_scale / mass
    rows = jnp.concatenate([lse, scale, jnp.zeros((128 - 2 * H, 128), jnp.float32)], axis=0).T

    for k in range(H):
        lk = logits[k * tb : (k + 1) * tb, :]
        tk = teach[k].astype(jnp.float32)
        student = jnp.exp(lk - rows[:, k : k + 1])
        delta[k * tb : (k + 1) * tb, :] = (loss_scale * student - tk * rows[:, H + k : H + k + 1]).astype(
            jnp.bfloat16
        )
        if (k + 1) % (H // nsub) == 0:
            send_delta((k + 1) // (H // nsub) - 1)

    for k in range(H):
        lk = logits[k * tb : (k + 1) * tb, :]
        tk = teach[k].astype(jnp.float32)
        live = tk > 0.0
        term = jnp.where(live, tk * (jnp.log(jnp.where(live, tk, 1.0)) - lk), 0.0)
        table = jnp.broadcast_to(jnp.sum(term, axis=1, keepdims=True), (tb, 128)).T
        terms[k : k + 1, :] = table[0:1, :]
    term_x = share(terms.at[...], term_in.at[0], s_tm.at[0], r_tm.at[0], X, x, to_x)
    term_y = share(terms.at[...], term_in.at[1], s_tm.at[1], r_tm.at[1], Y, y, to_y)
    term_x[0]()

    def term_z(o):
        zd = lax.rem(z + o, Z)
        return zd, rc(terms.at[...], term_in.at[2, Z - o], s_tz.at[lax.rem(zd, H)], r_tm.at[2], dev(x, y, c, zd))

    def terms_to_y():
        term_x[1]()
        summed(terms, term_in.at[0], X)
        term_y[0]()

    def terms_to_z():
        term_y[1]()
        summed(terms, term_in.at[1], Y)
        for o in order:
            zd, copy = term_z(o)

            @pl.when(lax.div(zd, H) == c)
            def _():
                copy.start()

    def finish_terms():
        for o in order:
            zd, copy = term_z(o)

            @pl.when(lax.div(zd, H) == c)
            def _():
                copy.wait_send()

        @pl.when(zh == c)
        def _():
            all_in = term_in.at[2, pl.ds(1, Z - 1)]
            pltpu.make_async_copy(all_in, all_in, r_tm.at[2]).wait()
            total = terms[0:H, :]
            for o in range(1, Z):
                total = total + term_in[2, o, 0:H, :]
            kl = total / mass - jnp.log(mass) + lse
            pick = lax.broadcasted_iota(jnp.int32, (H, 128), 0) == zl
            fin[0:1, :] = jnp.sum(jnp.where(pick, lse, 0.0), axis=0, keepdims=True)
            fin[1:2, :] = jnp.sum(jnp.where(pick, kl, 0.0), axis=0, keepdims=True)
            fi_copy.start()

    fi_copy = rc(fin.at[...], fin_in.at[...], s_fi, r_fi, partner)

    head_copy.wait()
    gt[...] = jnp.zeros_like(gt)
    pltpu.make_async_copy(hidt.at[pc], hidt.at[pc], r_ht).wait()

    def to_gt(kk):
        cols = pl.ds(pl.multiple_of(kk * cs, cs), cs)
        for h in range(2):
            gt[h] += lax.dot_general(
                head[:, cols], dg[kk, h].reshape(th, cs), (((1,), (1,)), ((), ())), preferred_element_type=jnp.float32
            )

    def to_ghead(kk):
        cols = pl.ds(pl.multiple_of(kk * cs, cs), cs)
        res[...] = jnp.dot(hidt[0], dg[kk, 0].reshape(th, cs), preferred_element_type=jnp.float32) + jnp.dot(
            hidt[1], dg[kk, 1].reshape(th, cs), preferred_element_type=jnp.float32
        )
        ghead[:, cols] = res[pl.ds(pl.multiple_of(off, 64), db), :].astype(jnp.bfloat16)

    def ghead_copy(kk):
        cols = pl.ds(pl.multiple_of(kk * cs, cs), cs)
        return pltpu.make_async_copy(ghead.at[:, cols], ghead_out.at[:, cols], s_gh)

    def dl_arrived(kk, part, i):
        pltpu.make_async_copy(dg.at[kk, part, i], dg.at[kk, part, i], r_dl.at[kk, part, i]).wait()

    def df_copy(kk, part, i, direction):
        to = lax.rem(z + 1, Z) if direction == 0 else lax.rem(z + Z - 1, Z)
        view = dg.at[kk, part, i]
        return rc(view, view, s_df.at[kk, part, i], r_dl.at[kk, part, i], dev(x, y, c, to))

    def hop_source(direction, s):
        return lax.rem(z - s + Z, Z) if direction == 0 else lax.rem(z + s, Z)

    for s in range(0, Z // 2 + 1):
        for i in range(nsub if s else 0):
            for part in range(2):
                for direction in range(2):
                    if s <= hops[part][direction]:
                        zs = hop_source(direction, s)
                        kk = lax.rem(zs, H)

                        @pl.when(lax.div(zs, H) == c)
                        def _():
                            dl_arrived(kk, part, i)
                            if s < hops[part][direction]:
                                df_copy(kk, part, i, direction).start()

        if s == 0:

            @pl.when(zh == c)
            def _():
                for part in range(2):
                    for i in range(nsub):
                        dl_arrived(zl, part, i)
                to_gt(zl)
        else:

            @pl.loop(0, 1 if 2 * s == Z else 2)
            def _(i):
                zs = lax.rem(z + Z - s + 2 * s * i, Z)

                @pl.when(lax.div(zs, H) == c)
                def _():
                    to_gt(lax.rem(zs, H))

        if s == 1:
            terms_to_y()
        if s == min(2, Z // 2):
            terms_to_z()

    nd = gx.shape[0]
    rows = db // nd
    sub = db // Y
    x_order = sorted(range(X), key=lambda o: -min(o, X - o))

    def gc_copy(dh, o):
        block = tokens_of(lax.rem(x + o, X), pc, z)
        lanes = pl.ds(pl.multiple_of(block * tb, tb), tb)
        return rc(
            gt.at[pc, pl.ds(dh * rows, rows), lanes], gc.at[dh, o], s_gc, r_gc.at[dh, o], partner
        )

    def gx_copy(dh, o):
        return rc(gsum.at[dh, o], gx.at[dh, X - o], s_gx, r_gx.at[dh], to_x(lax.rem(x + o, X)))

    for dh in range(nd):
        for o in x_order:
            gc_copy(dh, o).start()
    for dh in range(nd):
        for o in x_order:
            block = tokens_of(lax.rem(x + o, X), c, z)
            lanes = pl.ds(pl.multiple_of(block * tb, tb), tb)
            pltpu.make_async_copy(gc.at[dh, o], gc.at[dh, o], r_gc.at[dh, o]).wait()
            gsum[dh, o] = gt[c, dh * rows : (dh + 1) * rows, lanes] + gc[dh, o]
            if o:
                gx_copy(dh, o).start()

    @pl.loop(0, H)
    def _(kk):
        to_ghead(kk)
        ghead_copy(kk).start()

    finish_terms()

    def gy_copy(o):
        yd = lax.rem(y + o, Y)
        i = rows_of(yd, z)
        return i, rc(
            gx.at[lax.div(i * nd, Y), 0, pl.ds(pl.multiple_of(lax.rem(i, Y // nd) * sub, sub), sub), :],
            gy.at[Y - o],
            s_gy,
            r_gy,
            to_y(yd),
        )

    y_order = sorted(range(1, Y), key=lambda o: -min(o, Y - o))
    for dh in range(nd):
        acc = gsum[dh, 0]
        if X > 1:
            all_in = gx.at[dh, pl.ds(1, X - 1)]
            pltpu.make_async_copy(all_in, all_in, r_gx.at[dh]).wait()
        for o in range(1, X):
            acc = acc + gx[dh, o]
        gx[dh, 0] = acc
        for o in y_order:
            i, copy = gy_copy(o)

            @pl.when(lax.div(i * nd, Y) == dh)
            def _():
                copy.start()

    mine = rows_of(y, z)
    acc = gx[lax.div(mine * nd, Y), 0, pl.ds(pl.multiple_of(lax.rem(mine, Y // nd) * sub, sub), sub), :]
    if Y > 1:
        all_in = gy.at[pl.ds(1, Y - 1)]
        pltpu.make_async_copy(all_in, all_in, r_gy).wait()
    for o in range(1, Y):
        acc = acc + gy[o]
    gf[0] = acc

    go_copy = rc(gf.at[0], gf.at[1], s_go, r_go, {"vocab": vt, "tok": zt})
    go_local = pltpu.make_async_copy(gf.at[0], gf.at[1], r_go)

    @pl.when(at_home)
    def _():
        go_local.start()

    @pl.when(jnp.logical_not(at_home))
    def _():
        go_copy.start()

    @pl.when(zh == c)
    def _():
        fi_copy.wait_send()
        stat_out[...] = fin[...]

    @pl.when(zh != c)
    def _():
        pltpu.make_async_copy(fin_in.at[...], fin_in.at[...], r_fi).wait()
        stat_out[...] = fin_in[...]

    pltpu.make_async_copy(gc.at[...], gc.at[...], s_gc).wait()
    if X > 1:
        all_out = gx.at[:, pl.ds(1, X - 1)]
        pltpu.make_async_copy(all_out, all_out, s_gx).wait()
    if Y > 1:
        all_out = gy.at[pl.ds(1, Y - 1)]
        pltpu.make_async_copy(all_out, all_out, s_gy).wait()

    def drain(k0, kn, nrows, nlanes, sem):
        if min(kn, nrows, nlanes) > 0:
            view = hid.at[pl.ds(k0, kn), pl.ds(0, nrows), pl.ds(0, nlanes)]
            pltpu.make_async_copy(view, view, sem).wait()

    drain(0, split, pr, (X - 1) * plan, s_ga.at[0, 0])
    drain(0, split, (Y - 1) * pr, d, s_ga.at[0, 1])
    drain(split, H - split, (Y - 1) * pr, plan, s_ga.at[1, 0])
    drain(split, H - split, tb, (X - 1) * plan, s_ga.at[1, 1])
    for o in order:
        zd, copy = hz_copy(o)

        @pl.when(lax.div(zd, H) == c)
        def _():
            copy.wait_send()

        zd, copy = hd_copy(o)

        @pl.when(lax.div(zd, H) == c)
        def _():
            copy.wait_send()

        zd, copy = te_copy(o)

        @pl.when(lax.div(zd, H) == c)
        def _():
            copy.wait_send()

        zd, copy = mass_z(o)

        @pl.when(lax.div(zd, H) == c)
        def _():
            copy.wait_send()

        zs = lax.rem(z + o, Z)

        @pl.when(lax.div(zs, H) == c)
        def _():
            hf_copy(zs).wait_send()

    @pl.when(zh == c)
    def _():
        own_head.wait_send()

    ht_copy.wait_send()
    for i in range(nsub):
        dl_copy(0, i).wait_send()
        if both_ways:
            dl_copy(1, i).wait_send()
        else:

            @pl.when(c == 1)
            def _():
                dl_copy(1, i).wait_send()

        @pl.when(zh != c)
        def _():
            dl_local(i).wait_send()

        for s in range(1, Z // 2 + 1):
            for part in range(2):
                for direction in range(2):
                    if s < hops[part][direction]:
                        zs = hop_source(direction, s)

                        @pl.when(lax.div(zs, H) == c)
                        def _():
                            df_copy(lax.rem(zs, H), part, i, direction).wait_send()

    @pl.when(jnp.logical_not(at_home))
    def _():
        go_copy.wait_send()

    pltpu.make_async_copy(ghead, ghead_out, s_gh).wait()

    go_local.wait()
    ghid_out[...] = gf[1]


def per_device(geo, hidden, head, teacher, block_ids, counts):
    X, Y, Z, blk = geo
    H = Z // 2
    tb, d = hidden.shape
    db, cb = head.shape
    cs, th = cb // H, tb * H
    win = -(-db // 128) * 128
    sub = db // Y
    f32, bf16 = jnp.float32, jnp.bfloat16
    dma = pltpu.SemaphoreType.DMA
    most = max(X, Y)
    half = max(most // 2, 1)
    nd = 2 if Y % 2 == 0 else 1
    nsub = 2 if H % 2 == 0 else 1
    scratch = [
        pltpu.VMEM((db, cb), bf16),
        pltpu.VMEM((tb, cb), bf16),
        pltpu.VMEM((tb, cb), bf16),
        pltpu.VMEM((H, tb, d), bf16),
        pltpu.VMEM((Z, db, cs), bf16),
        pltpu.VMEM((H, tb, cs), bf16),
        pltpu.VMEM((th, cs), f32),
        pltpu.VMEM((8, 128), f32),
        pltpu.VMEM((3, max(X, Y), 8, 128), f32),
        pltpu.VMEM((H, 8, 128), f32),
        pltpu.VMEM((8, 128), f32),
        pltpu.VMEM((3, max(X, Y, Z), 8, 128), f32),
        pltpu.VMEM((2 * H, 128), f32),
        pltpu.VMEM((3, max(X, Y, Z), 2 * H, 128), f32),
        pltpu.VMEM((th, cs), bf16),
        pltpu.VMEM((H, 2, nsub, th // nsub, cs), bf16),
        pltpu.VMEM((2, win, th), bf16),
        pltpu.VMEM((win, cs), f32),
        pltpu.VMEM((db, cb), bf16),
        pltpu.VMEM((2, db, th), f32),
        pltpu.VMEM((nd, X, db // nd, tb), f32),
        pltpu.VMEM((nd, X, db // nd, tb), f32),
        pltpu.VMEM((Y, sub, tb), f32),
        pltpu.VMEM((2, sub, tb), f32),
        pltpu.VMEM((nd, X, db // nd, tb), f32),
        pltpu.VMEM((8, 128), f32),
        pltpu.VMEM((8, 128), f32),
        dma((2,)), dma,
        dma((H,)), dma((H,)),
        dma((2, 2)), dma((2, 2, half)), dma((2, max(X * Y, 2 * X, 2 * Y))),
        dma((Z,)), dma((H,)), dma((Z,)),
        dma((H,)), dma((H,)),
        dma((3,)), dma((3,)),
        dma((H,)), dma((H,)),
        dma((2,)), dma((3,)), dma((H,)),
        dma((3,)), dma((3,)),
        dma((3, nsub)), dma((H, 2, nsub)), dma((H, 2, nsub)),
        dma, dma,
        dma, dma((nd, X)),
        dma, dma((nd,)),
        dma, dma,
        dma, dma,
        dma, dma,
    ]
    vm = pl.BlockSpec(memory_space=pltpu.VMEM)
    hbm = pl.BlockSpec(memory_space=pl.ANY)
    sm = pl.BlockSpec(memory_space=pltpu.SMEM)
    ghead, ghid, stats = pl.pallas_call(
        functools.partial(kernel_body, geo),
        out_shape=(
            jax.ShapeDtypeStruct((db, cb), bf16),
            jax.ShapeDtypeStruct((sub, tb), f32),
            jax.ShapeDtypeStruct((8, 128), f32),
        ),
        in_specs=[hbm, hbm, hbm, sm, sm],
        out_specs=(hbm, vm, vm),
        scratch_shapes=scratch,
        compiler_params=pltpu.CompilerParams(has_side_effects=True, collective_id=0, vmem_limit_bytes=60 * 2**20),
    )(hidden, head, teacher, block_ids, counts)

    def place(
        stats_in, ghid_in, ghead_in, lse_to, kl_to, ghid_to, ghead_to, stats_at, ghid_at, ghead_at, in_sem, out_sem
    ):
        moves = [(stats_in, stats_at), (ghid_in, ghid_at)]
        parts = [pl.ds(k * cs, cs) for k in range(H)]
        moves += [(ghead_in.at[:, part], ghead_at.at[:, part]) for part in parts]
        loads = [pltpu.make_async_copy(src, dst, in_sem.at[k]) for k, (src, dst) in enumerate(moves)]
        for load in loads:
            load.start()
        loads[0].wait()
        stores = [
            pltpu.make_async_copy(stats_at.at[pl.ds(0, 1)], lse_to, out_sem.at[0]),
            pltpu.make_async_copy(stats_at.at[pl.ds(1, 1)], kl_to, out_sem.at[1]),
        ]
        stores[0].start()
        stores[1].start()
        loads[1].wait()
        stores.append(pltpu.make_async_copy(ghid_at, ghid_to, out_sem.at[2]))
        stores[2].start()
        for k, part in enumerate(parts):
            loads[2 + k].wait()
            stores.append(pltpu.make_async_copy(ghead_at.at[:, part], ghead_to.at[:, part], out_sem.at[3 + k]))
            stores[3 + k].start()
        for store in stores:
            store.wait()

    lse, kl, ghid, ghead = pl.pallas_call(
        place,
        out_shape=(
            jax.ShapeDtypeStruct((1, tb), f32),
            jax.ShapeDtypeStruct((1, tb), f32),
            jax.ShapeDtypeStruct(ghid.shape, f32),
            jax.ShapeDtypeStruct(ghead.shape, bf16),
        ),
        in_specs=[hbm, hbm, hbm],
        out_specs=(hbm, hbm, hbm, hbm),
        scratch_shapes=[
            pltpu.VMEM((8, 128), f32),
            pltpu.VMEM(ghid.shape, f32),
            pltpu.VMEM(ghead.shape, bf16),
            dma((2 + H,)),
            dma((3 + H,)),
        ],
    )(stats, ghid, ghead)
    return lse.reshape(tb), kl.reshape(tb), ghid.T, ghead


def solution(mesh, ring_y=RING_Y, blk=BLK):
    vocab, tok = mesh.shape["vocab"], mesh.shape["tok"]
    geo = (vocab // (2 * ring_y), ring_y, tok, blk)
    placed = (P("tok", None), P("tok", "vocab"), P("tok", "vocab"), P("tok", None), P("tok"))
    return jax.shard_map(
        functools.partial(per_device, geo),
        mesh=mesh,
        in_specs=placed,
        out_specs=(P("tok"), P("tok"), P("tok", "vocab"), P("tok", "vocab")),
        check_vma=False,
    )
```

```python
import functools

import jax
import jax.numpy as jnp
from jax import lax
from jax.experimental import pallas as pl
from jax.experimental.pallas import tpu as pltpu
from jax.sharding import PartitionSpec as P

BLK = 512
RING_Y = 8

MESH = pl.DeviceIdType.MESH
loss_scale = 1024.0


def ring_hops(n, parts):
    if parts == 1:
        return [(n // 2, (n - 1) // 2)]
    return [(n // 2, (n - 1) // 2), ((n - 1) // 2, n // 2)]


def kernel_body(
    geo,
    hidden, head_in, teacher_in, ids, counts,
    ghead_out, ghid_out, stat_out,
    head, teacher, kept, hid, headt, teach, logits, masses, mass_in, mass_of, terms, term_in, stat, stat_in, delta, dg, hidt, res, ghead, gt, gc, gx, gy, gf, gsum, fin, fin_in,
    s_in, s_gh, s_hz, r_hz, s_ga, r_ga, r_gb, s_hd, s_hf, r_hd, s_te, r_te, s_ms, r_ms, s_mz, r_mz, s_tm, r_tm, s_tz, s_st, r_st, s_dl, s_df, r_dl, s_ht, r_ht,
    s_gc, r_gc, s_gx, r_gx, s_gy, r_gy, s_go, r_go, s_fi, r_fi,
):
    X, Y, Z, blk = geo
    H = Z // 2
    tb, d = hidden.shape
    db, cb = head_in.shape
    cs = cb // H
    th = tb * H
    v = lax.axis_index("vocab")
    z = lax.axis_index("tok")
    c = lax.rem(v, 2)
    y = lax.rem(lax.div(v, 2), Y)
    x = lax.div(v, 2 * Y)
    zh, zl = lax.div(z, H), lax.rem(z, H)
    pc = 1 - c

    def dev(xx, yy, cc, zz):
        return {"vocab": (xx * Y + yy) * 2 + cc, "tok": zz}

    def rc(src, dst, ssem, rsem, device):
        return pltpu.make_async_remote_copy(
            src_ref=src, dst_ref=dst, send_sem=ssem, recv_sem=rsem, device_id=device, device_id_type=MESH
        )

    partner = dev(x, y, pc, z)

    def rows_of(yy, zz):
        return lax.rem(yy + Y // 4 + (Y // 2) * lax.rem(zz, 2), Y)

    def tokens_of(xx, cc, zz):
        same = lax.rem(cc + lax.div(zz, H) + 1, 2)
        return lax.rem(lax.rem(zz, H) + xx + X - lax.div(zz, 2) + (H // 2) * same, H)

    vt, zt = z * Y + rows_of(y, z), c * H + tokens_of(x, c, z)
    at_home = (vt == v) & (zt == z)
    zs_home, cs_home = lax.div(v, Y), zh
    same_home = lax.rem(cs_home + lax.div(zs_home, H) + 1, 2)
    ys_home = lax.rem(lax.rem(v, Y) + 2 * Y - Y // 4 - (Y // 2) * lax.rem(zs_home, 2), Y)
    xs_home = lax.rem(zl + 2 * H - lax.rem(zs_home, H) - (H // 2) * same_home + lax.div(zs_home, 2), X)
    vs = (xs_home * Y + ys_home) * 2 + cs_home

    barrier = pltpu.get_barrier_semaphore()

    def greet(device):
        pl.semaphore_signal(barrier, inc=1, device_id=device, device_id_type=MESH)

    greet(partner)
    for o in range(1, Z):
        for cc in range(2):
            greet(dev(x, y, cc, lax.rem(z + o, Z)))
    for o in range(1, X):
        greet(dev(lax.rem(x + o, X), y, c, z))
    for o in range(1, Y):
        greet(dev(x, lax.rem(y + o, Y), c, z))

    @pl.when(jnp.logical_not(at_home))
    def _():
        greet({"vocab": vt, "tok": zt})
        greet({"vocab": vs, "tok": zs_home})

    head_copy = pltpu.make_async_copy(head_in, head, s_in.at[0])
    teacher_copy = pltpu.make_async_copy(teacher_in, teacher, s_in.at[1])
    teacher_copy.start()
    head_copy.start()

    near = 1 + 2 * (Z - 1) + (X - 1) + (Y - 1)
    pl.semaphore_wait(barrier, jnp.where(at_home, near, near + 2))

    order = sorted(range(1, Z), key=lambda o: min(o, Z - o))

    pr, plan = tb // Y, d // X
    row0 = pl.multiple_of(y * pr, pr)
    lane0 = pl.multiple_of(x * plan, plan)
    piece = hidden.at[pl.ds(row0, pr), pl.ds(lane0, plan)]
    piece_to = hid.at[zl, pl.ds(row0, pr), pl.ds(lane0, plan)]

    def hz_copy(o):
        zd = lax.rem(z + o, Z)
        return zd, rc(piece, piece_to, s_hz.at[lax.rem(zd, H)], r_hz.at[zl], dev(x, y, zh, zd))

    for o in order:
        zd, copy = hz_copy(o)

        @pl.when(lax.div(zd, H) == c)
        def _():
            copy.start()

    @pl.when(zh == c)
    def _():
        pltpu.make_async_copy(piece, piece_to, r_hz.at[zl]).start()

    def hd_copy(o):
        zd = lax.rem(z + o, Z)
        cols = pl.ds(pl.multiple_of(lax.rem(zd, H) * cs, cs), cs)
        return zd, rc(head_in.at[:, cols], headt.at[z], s_hd.at[o], r_hd.at[z], dev(x, y, zh, zd))

    for o in order:
        zd, copy = hd_copy(o)

        @pl.when(lax.div(zd, H) == c)
        def _():
            copy.start()

    own_cols = pl.ds(pl.multiple_of(zl * cs, cs), cs)

    own_head = rc(head_in.at[:, own_cols], headt.at[z], s_hd.at[0], r_hd.at[z], partner)

    @pl.when(zh == c)
    def _():
        pltpu.make_async_copy(head_in.at[:, own_cols], headt.at[z], r_hd.at[z]).start()
        own_head.start()

    slots = ids.shape[1]
    teacher_copy.wait()
    local_mass = jnp.zeros((tb, 1), jnp.float32)
    for k in range(cb // blk):
        block = v * (cb // blk) + k
        hit = jnp.int32(0)
        for s in range(slots):
            hit = hit | jnp.where((ids[0, s] == block) & (s < counts[0]), 1, 0)
        part = teacher[:, k * blk : (k + 1) * blk]
        keep = jnp.full(part.shape, hit, jnp.int32) > 0
        part = jnp.where(keep, part.astype(jnp.float32), 0.0)
        kept[:, k * blk : (k + 1) * blk] = part.astype(jnp.bfloat16)
        local_mass = local_mass + jnp.sum(part, axis=1, keepdims=True)

    def te_copy(o):
        zd = lax.rem(z + o, Z)
        cols = pl.ds(pl.multiple_of(lax.rem(zd, H) * cs, cs), cs)
        return zd, rc(kept.at[:, cols], teach.at[zl], s_te.at[lax.rem(zd, H)], r_te.at[zl], dev(x, y, zh, zd))

    for o in order:
        zd, copy = te_copy(o)

        @pl.when(lax.div(zd, H) == c)
        def _():
            copy.start()

    @pl.when(zh == c)
    def _():
        pltpu.make_async_copy(kept.at[:, own_cols], teach.at[zl], r_te.at[zl]).start()

    masses[...] = jnp.broadcast_to(local_mass, (tb, 128)).T[0:8, :]

    def share(buffer, inbox, ssem, rsem, n, me, to):
        def start():
            for o in range(1, n):
                rc(buffer, inbox.at[n - o], ssem, rsem, to(lax.rem(me + o, n))).start()

        def arrive():
            if n > 1:
                all_in = inbox.at[pl.ds(1, n - 1)]
                pltpu.make_async_copy(all_in, all_in, ssem).wait()
                pltpu.make_async_copy(all_in, all_in, rsem).wait()

        return start, arrive

    def to_x(i):
        return dev(i, y, c, z)

    def to_y(i):
        return dev(x, i, c, z)

    def summed(buffer, inbox, n):
        total = buffer[...]
        for o in range(1, n):
            total = total + inbox[o]
        buffer[...] = total

    mass_c = rc(masses.at[...], mass_in.at[0, 0], s_ms.at[0], r_ms.at[0], partner)
    mass_x = share(masses.at[...], mass_in.at[1], s_ms.at[1], r_ms.at[1], X, x, to_x)
    mass_y = share(masses.at[...], mass_in.at[2], s_ms.at[2], r_ms.at[2], Y, y, to_y)
    mass_c.start()
    mass_c.wait()
    masses[...] = masses[...] + mass_in[0, 0]
    mass_x[0]()

    def gather(g, planes, first, second, block):
        (n1, me1, to1), (n2, me2, to2) = first, second
        hops1 = ring_hops(n1, 1)[0]

        def along(n, me, direction, s, to):
            source = lax.rem(me - (s - 1) + n, n) if direction == 0 else lax.rem(me + (s - 1), n)
            target = lax.rem(me + 1, n) if direction == 0 else lax.rem(me + n - 1, n)
            return source, to(target)

        def came(n, me, direction, s):
            return lax.rem(me - s + n, n) if direction == 0 else lax.rem(me + s, n)

        def send1(direction, s):
            source, device = along(n1, me1, direction, s, to1)
            view = block(source, me2)
            rc(view, view, s_ga.at[g, 0], r_ga.at[g, direction, s - 1], device).start()

        def wait1(direction, s):
            view = block(came(n1, me1, direction, s), me2)
            pltpu.make_async_copy(view, view, r_ga.at[g, direction, s - 1]).wait()

        def hops2(q):
            right, left = ring_hops(n2, 1)[0]
            return (right, left) if q % 2 == 0 else (left, right)

        def send2(q, direction, s):
            source, device = along(n2, me2, direction, s, to2)
            view = block(lax.rem(me1 + q, n1), source)
            rc(view, view, s_ga.at[g, 1], r_gb.at[g, (2 * q + direction) * (n2 // 2) + s - 1], device).start()

        for k in planes:
            pltpu.make_async_copy(piece, hid.at[k, pl.ds(row0, pr), pl.ds(lane0, plan)], r_hz.at[k]).wait()

        progress = {}

        def begin2(q):
            progress[q] = 1
            for direction in range(2):
                if hops2(q)[direction] >= 1:
                    send2(q, direction, 1)

        def advance2(q):
            s = progress[q]
            progress[q] += 1
            for direction in range(2):
                if s <= hops2(q)[direction]:
                    view = block(lax.rem(me1 + q, n1), came(n2, me2, direction, s))
                    pltpu.make_async_copy(view, view, r_gb.at[g, (2 * q + direction) * (n2 // 2) + s - 1]).wait()
                    if s < hops2(q)[direction]:
                        send2(q, direction, s + 1)

        for direction in range(2):
            if hops1[direction] >= 1:
                send1(direction, 1)
        begin2(0)
        yield
        for s in range(1, n1 // 2 + 1):
            earlier = list(progress)
            for direction in range(2):
                if s <= hops1[direction]:
                    wait1(direction, s)
                    if s < hops1[direction]:
                        send1(direction, s + 1)
                    begin2(n1 - s if direction == 0 else s)
            yield
            for q in earlier:
                if progress[q] <= n2 // 2:
                    advance2(q)
                    yield
        while any(at <= n2 // 2 for at in progress.values()):
            for q in list(progress):
                if progress[q] <= n2 // 2:
                    advance2(q)
                    yield
    def rows_at(i):
        return pl.ds(pl.multiple_of(i * pr, pr), pr)

    def lanes_at(i):
        return pl.ds(pl.multiple_of(i * plan, plan), plan)

    def hf_copy(zs):
        return rc(headt.at[zs], headt.at[zs], s_hf.at[lax.rem(zs, H)], r_hd.at[zs], partner)

    def head_arrived(zs):
        pltpu.make_async_copy(headt.at[zs], headt.at[zs], r_hd.at[zs]).wait()

    def head_onward(o):
        zs = lax.rem(z + o, Z)

        @pl.when(lax.div(zs, H) == c)
        def _():
            head_arrived(zs)
            hf_copy(zs).start()

    early = Z // 4
    split = H if H == 1 else H // 2
    x_first = gather(
        0, range(split), (X, x, to_x), (Y, y, to_y), lambda i, j: hid.at[pl.ds(0, split), rows_at(j), lanes_at(i)]
    )
    y_first = gather(
        1, range(split, H), (Y, y, to_y), (X, x, to_x), lambda i, j: hid.at[pl.ds(split, H - split), rows_at(i), lanes_at(j)]
    )
    todo = [x_first] if split == H else [x_first, y_first]
    turn = 0
    while todo:
        todo = [walk for walk in todo if next(walk, todo) is not todo]
        turn += 1
        if turn == 8:
            mass_x[1]()
            summed(masses, mass_in.at[1], X)
            mass_y[0]()
    if turn < 8:
        mass_x[1]()
        summed(masses, mass_in.at[1], X)
        mass_y[0]()
    for o in range(1, early + 1):
        head_onward(o)
        head_onward(Z - o)

    mass_y[1]()
    summed(masses, mass_in.at[2], Y)

    def mass_z(o):
        zd = lax.rem(z + o, Z)
        return zd, rc(masses, mass_of.at[zl], s_mz.at[lax.rem(zd, H)], r_mz.at[zl], dev(x, y, zh, zd))

    for o in order:
        zd, copy = mass_z(o)

        @pl.when(lax.div(zd, H) == c)
        def _():
            copy.start()

    @pl.when(zh == c)
    def _():
        pltpu.make_async_copy(masses, mass_of.at[zl], r_mz.at[zl]).start()

    win = hidt.shape[1]
    win0 = lax.div(z * db, 128) * 128
    off = z * db - win0
    for k in range(H):
        block = hid[k, :, pl.ds(pl.multiple_of(win0, 128), win)]
        hidt[c, :, k * tb : (k + 1) * tb] = block.T
    ht_copy = rc(hidt.at[c], hidt.at[c], s_ht, r_ht, partner)
    ht_copy.start()

    logits[...] = jnp.zeros_like(logits)
    kd = 2 * db
    for step in [0] + [q * sign for q in range(1, H // 2 + 1) for sign in (1, -1)][: H - 1]:
        p = lax.rem(lax.div(z, 2) + step + H, H)
        for zs in (2 * p, 2 * p + 1):

            away = lax.rem(zs - z + Z, Z)
            passed = (away != 0) & ((away <= early) | (away >= Z - early)) & (lax.div(zs, H) == c)
            onward = (away > early) & (away < Z - early) & (lax.div(zs, H) == c)

            @pl.when(jnp.logical_not(passed))
            def _():
                head_arrived(zs)

            @pl.when(onward)
            def _():
                hf_copy(zs).start()

        lhs = hid[:, :, pl.ds(pl.multiple_of(p * kd, 128), kd)].reshape(th, kd)
        rhs = headt[pl.ds(2 * p, 2)].reshape(kd, cs)
        logits[...] += jnp.dot(lhs, rhs, preferred_element_type=jnp.float32)

    lane = lax.broadcasted_iota(jnp.int32, (tb, 128), 1)

    for k in range(H):
        lk = logits[k * tb : (k + 1) * tb, :]
        top = jnp.max(lk, axis=1, keepdims=True)
        total = jnp.sum(jnp.exp(lk - top), axis=1, keepdims=True)
        table = jnp.where(lane == 0, top, total).T
        stat[k : k + 1, :] = table[0:1, :]
        stat[H + k : H + k + 1, :] = table[1:2, :]

    def exchange(stage, n, me, to):
        start, arrive = share(stat.at[...], stat_in.at[stage], s_st.at[stage], r_st.at[stage], n, me, to)
        start()
        arrive()
        blocks = [stat[...]] + [stat_in[stage, o] for o in range(1, n)]
        top = functools.reduce(jnp.maximum, [b[0:H] for b in blocks])
        total = functools.reduce(jnp.add, [b[H : 2 * H] * jnp.exp(b[0:H] - top) for b in blocks])
        stat[0:H, :] = top
        stat[H : 2 * H, :] = total

    exchange(0, X, x, to_x)
    exchange(1, Y, y, to_y)
    exchange(2, Z, z, lambda i: dev(x, y, c, i))

    for k in range(H):
        pltpu.make_async_copy(teach.at[k], teach.at[k], r_te.at[k]).wait()

    hops = ring_hops(Z, 2)
    nsub = dg.shape[2]
    tsub = th // nsub

    def dl_copy(direction, i):
        to = lax.rem(z + 1, Z) if direction == 0 else lax.rem(z + Z - 1, Z)
        return rc(
            delta.at[pl.ds(i * tsub, tsub)],
            dg.at[zl, c, i],
            s_dl.at[direction, i],
            r_dl.at[zl, c, i],
            dev(x, y, zh, to),
        )

    def dl_local(i):
        return rc(delta.at[pl.ds(i * tsub, tsub)], dg.at[zl, c, i], s_dl.at[2, i], r_dl.at[zl, c, i], partner)

    both_ways = min(hops[0] + hops[1]) > 0

    def send_delta(i):
        dl_copy(0, i).start()
        if both_ways:
            dl_copy(1, i).start()
        else:

            @pl.when(c == 1)
            def _():
                dl_copy(1, i).start()

        @pl.when(zh != c)
        def _():
            dl_local(i).start()

        @pl.when(zh == c)
        def _():
            pltpu.make_async_copy(delta.at[pl.ds(i * tsub, tsub)], dg.at[zl, c, i], r_dl.at[zl, c, i]).start()

    final = stat[...]
    lse = final[0:H] + jnp.log(final[H : 2 * H])
    for k in range(H):
        pltpu.make_async_copy(mass_of.at[k], mass_of.at[k], r_mz.at[k]).wait()
    mass = jnp.concatenate([mass_of[k, 0:1, :] for k in range(H)], axis=0)
    scale = loss_scale / mass
    rows = jnp.concatenate([lse, scale, jnp.zeros((128 - 2 * H, 128), jnp.float32)], axis=0).T

    for k in range(H):
        lk = logits[k * tb : (k + 1) * tb, :]
        tk = teach[k].astype(jnp.float32)
        student = jnp.exp(lk - rows[:, k : k + 1])
        delta[k * tb : (k + 1) * tb, :] = (loss_scale * student - tk * rows[:, H + k : H + k + 1]).astype(
            jnp.bfloat16
        )
        if (k + 1) % (H // nsub) == 0:
            send_delta((k + 1) // (H // nsub) - 1)

    for k in range(H):
        lk = logits[k * tb : (k + 1) * tb, :]
        tk = teach[k].astype(jnp.float32)
        live = tk > 0.0
        term = jnp.where(live, tk * (jnp.log(jnp.where(live, tk, 1.0)) - lk), 0.0)
        table = jnp.broadcast_to(jnp.sum(term, axis=1, keepdims=True), (tb, 128)).T
        terms[k : k + 1, :] = table[0:1, :]
    term_x = share(terms.at[...], term_in.at[0], s_tm.at[0], r_tm.at[0], X, x, to_x)
    term_y = share(terms.at[...], term_in.at[1], s_tm.at[1], r_tm.at[1], Y, y, to_y)
    term_x[0]()

    def term_z(o):
        zd = lax.rem(z + o, Z)
        return zd, rc(terms.at[...], term_in.at[2, Z - o], s_tz.at[lax.rem(zd, H)], r_tm.at[2], dev(x, y, c, zd))

    def terms_to_y():
        term_x[1]()
        summed(terms, term_in.at[0], X)
        term_y[0]()

    def terms_to_z():
        term_y[1]()
        summed(terms, term_in.at[1], Y)
        for o in order:
            zd, copy = term_z(o)

            @pl.when(lax.div(zd, H) == c)
            def _():
                copy.start()

    def finish_terms():
        for o in order:
            zd, copy = term_z(o)

            @pl.when(lax.div(zd, H) == c)
            def _():
                copy.wait_send()

        @pl.when(zh == c)
        def _():
            all_in = term_in.at[2, pl.ds(1, Z - 1)]
            pltpu.make_async_copy(all_in, all_in, r_tm.at[2]).wait()
            total = terms[0:H, :]
            for o in range(1, Z):
                total = total + term_in[2, o, 0:H, :]
            kl = total / mass - jnp.log(mass) + lse
            pick = lax.broadcasted_iota(jnp.int32, (H, 128), 0) == zl
            fin[0:1, :] = jnp.sum(jnp.where(pick, lse, 0.0), axis=0, keepdims=True)
            fin[1:2, :] = jnp.sum(jnp.where(pick, kl, 0.0), axis=0, keepdims=True)
            fi_copy.start()

    fi_copy = rc(fin.at[...], fin_in.at[...], s_fi, r_fi, partner)

    head_copy.wait()
    gt[...] = jnp.zeros_like(gt)
    pltpu.make_async_copy(hidt.at[pc], hidt.at[pc], r_ht).wait()

    def to_gt(kk):
        cols = pl.ds(pl.multiple_of(kk * cs, cs), cs)
        for h in range(2):
            gt[h] += lax.dot_general(
                head[:, cols], dg[kk, h].reshape(th, cs), (((1,), (1,)), ((), ())), preferred_element_type=jnp.float32
            )

    def to_ghead(kk):
        cols = pl.ds(pl.multiple_of(kk * cs, cs), cs)
        res[...] = jnp.dot(hidt[0], dg[kk, 0].reshape(th, cs), preferred_element_type=jnp.float32) + jnp.dot(
            hidt[1], dg[kk, 1].reshape(th, cs), preferred_element_type=jnp.float32
        )
        ghead[:, cols] = res[pl.ds(pl.multiple_of(off, 64), db), :].astype(jnp.bfloat16)

    def ghead_copy(kk):
        cols = pl.ds(pl.multiple_of(kk * cs, cs), cs)
        return pltpu.make_async_copy(ghead.at[:, cols], ghead_out.at[:, cols], s_gh)

    def dl_arrived(kk, part, i):
        pltpu.make_async_copy(dg.at[kk, part, i], dg.at[kk, part, i], r_dl.at[kk, part, i]).wait()

    def df_copy(kk, part, i, direction):
        to = lax.rem(z + 1, Z) if direction == 0 else lax.rem(z + Z - 1, Z)
        view = dg.at[kk, part, i]
        return rc(view, view, s_df.at[kk, part, i], r_dl.at[kk, part, i], dev(x, y, c, to))

    def hop_source(direction, s):
        return lax.rem(z - s + Z, Z) if direction == 0 else lax.rem(z + s, Z)

    for s in range(0, Z // 2 + 1):
        for i in range(nsub if s else 0):
            for part in range(2):
                for direction in range(2):
                    if s <= hops[part][direction]:
                        zs = hop_source(direction, s)
                        kk = lax.rem(zs, H)

                        @pl.when(lax.div(zs, H) == c)
                        def _():
                            dl_arrived(kk, part, i)
                            if s < hops[part][direction]:
                                df_copy(kk, part, i, direction).start()

        if s == 0:

            @pl.when(zh == c)
            def _():
                for part in range(2):
                    for i in range(nsub):
                        dl_arrived(zl, part, i)
                to_gt(zl)
        else:

            @pl.loop(0, 1 if 2 * s == Z else 2)
            def _(i):
                zs = lax.rem(z + Z - s + 2 * s * i, Z)

                @pl.when(lax.div(zs, H) == c)
                def _():
                    to_gt(lax.rem(zs, H))

        if s == 1:
            terms_to_y()
        if s == min(2, Z // 2):
            terms_to_z()

    nd = gx.shape[0]
    rows = db // nd
    sub = db // Y
    x_order = sorted(range(X), key=lambda o: -min(o, X - o))

    def gc_copy(dh, o):
        block = tokens_of(lax.rem(x + o, X), pc, z)
        lanes = pl.ds(pl.multiple_of(block * tb, tb), tb)
        return rc(
            gt.at[pc, pl.ds(dh * rows, rows), lanes], gc.at[dh, o], s_gc, r_gc.at[dh, o], partner
        )

    def gx_copy(dh, o):
        return rc(gsum.at[dh, o], gx.at[dh, X - o], s_gx, r_gx.at[dh], to_x(lax.rem(x + o, X)))

    for dh in range(nd):
        for o in x_order:
            gc_copy(dh, o).start()
    for dh in range(nd):
        for o in x_order:
            block = tokens_of(lax.rem(x + o, X), c, z)
            lanes = pl.ds(pl.multiple_of(block * tb, tb), tb)
            pltpu.make_async_copy(gc.at[dh, o], gc.at[dh, o], r_gc.at[dh, o]).wait()
            gsum[dh, o] = gt[c, dh * rows : (dh + 1) * rows, lanes] + gc[dh, o]
            if o:
                gx_copy(dh, o).start()

    @pl.loop(0, H)
    def _(kk):
        to_ghead(kk)
        ghead_copy(kk).start()

    finish_terms()

    def gy_copy(o):
        yd = lax.rem(y + o, Y)
        i = rows_of(yd, z)
        return i, rc(
            gx.at[lax.div(i * nd, Y), 0, pl.ds(pl.multiple_of(lax.rem(i, Y // nd) * sub, sub), sub), :],
            gy.at[Y - o],
            s_gy,
            r_gy,
            to_y(yd),
        )

    y_order = sorted(range(1, Y), key=lambda o: -min(o, Y - o))
    for dh in range(nd):
        acc = gsum[dh, 0]
        if X > 1:
            all_in = gx.at[dh, pl.ds(1, X - 1)]
            pltpu.make_async_copy(all_in, all_in, r_gx.at[dh]).wait()
        for o in range(1, X):
            acc = acc + gx[dh, o]
        gx[dh, 0] = acc
        for o in y_order:
            i, copy = gy_copy(o)

            @pl.when(lax.div(i * nd, Y) == dh)
            def _():
                copy.start()

    mine = rows_of(y, z)
    acc = gx[lax.div(mine * nd, Y), 0, pl.ds(pl.multiple_of(lax.rem(mine, Y // nd) * sub, sub), sub), :]
    if Y > 1:
        all_in = gy.at[pl.ds(1, Y - 1)]
        pltpu.make_async_copy(all_in, all_in, r_gy).wait()
    for o in range(1, Y):
        acc = acc + gy[o]
    gf[0] = acc

    go_copy = rc(gf.at[0], gf.at[1], s_go, r_go, {"vocab": vt, "tok": zt})
    go_local = pltpu.make_async_copy(gf.at[0], gf.at[1], r_go)

    @pl.when(at_home)
    def _():
        go_local.start()

    @pl.when(jnp.logical_not(at_home))
    def _():
        go_copy.start()

    @pl.when(zh == c)
    def _():
        fi_copy.wait_send()
        stat_out[...] = fin[...]

    @pl.when(zh != c)
    def _():
        pltpu.make_async_copy(fin_in.at[...], fin_in.at[...], r_fi).wait()
        stat_out[...] = fin_in[...]

    pltpu.make_async_copy(gc.at[...], gc.at[...], s_gc).wait()
    if X > 1:
        all_out = gx.at[:, pl.ds(1, X - 1)]
        pltpu.make_async_copy(all_out, all_out, s_gx).wait()
    if Y > 1:
        all_out = gy.at[pl.ds(1, Y - 1)]
        pltpu.make_async_copy(all_out, all_out, s_gy).wait()

    def drain(k0, kn, nrows, nlanes, sem):
        if min(kn, nrows, nlanes) > 0:
            view = hid.at[pl.ds(k0, kn), pl.ds(0, nrows), pl.ds(0, nlanes)]
            pltpu.make_async_copy(view, view, sem).wait()

    drain(0, split, pr, (X - 1) * plan, s_ga.at[0, 0])
    drain(0, split, (Y - 1) * pr, d, s_ga.at[0, 1])
    drain(split, H - split, (Y - 1) * pr, plan, s_ga.at[1, 0])
    drain(split, H - split, tb, (X - 1) * plan, s_ga.at[1, 1])
    for o in order:
        zd, copy = hz_copy(o)

        @pl.when(lax.div(zd, H) == c)
        def _():
            copy.wait_send()

        zd, copy = hd_copy(o)

        @pl.when(lax.div(zd, H) == c)
        def _():
            copy.wait_send()

        zd, copy = te_copy(o)

        @pl.when(lax.div(zd, H) == c)
        def _():
            copy.wait_send()

        zd, copy = mass_z(o)

        @pl.when(lax.div(zd, H) == c)
        def _():
            copy.wait_send()

        zs = lax.rem(z + o, Z)

        @pl.when(lax.div(zs, H) == c)
        def _():
            hf_copy(zs).wait_send()

    @pl.when(zh == c)
    def _():
        own_head.wait_send()

    ht_copy.wait_send()
    for i in range(nsub):
        dl_copy(0, i).wait_send()
        if both_ways:
            dl_copy(1, i).wait_send()
        else:

            @pl.when(c == 1)
            def _():
                dl_copy(1, i).wait_send()

        @pl.when(zh != c)
        def _():
            dl_local(i).wait_send()

        for s in range(1, Z // 2 + 1):
            for part in range(2):
                for direction in range(2):
                    if s < hops[part][direction]:
                        zs = hop_source(direction, s)

                        @pl.when(lax.div(zs, H) == c)
                        def _():
                            df_copy(lax.rem(zs, H), part, i, direction).wait_send()

    @pl.when(jnp.logical_not(at_home))
    def _():
        go_copy.wait_send()

    pltpu.make_async_copy(ghead, ghead_out, s_gh).wait()

    go_local.wait()
    ghid_out[...] = gf[1]


def per_device(geo, hidden, head, teacher, block_ids, counts):
    X, Y, Z, blk = geo
    H = Z // 2
    tb, d = hidden.shape
    db, cb = head.shape
    cs, th = cb // H, tb * H
    win = -(-db // 128) * 128
    sub = db // Y
    f32, bf16 = jnp.float32, jnp.bfloat16
    dma = pltpu.SemaphoreType.DMA
    most = max(X, Y)
    half = max(most // 2, 1)
    nd = 2 if Y % 2 == 0 else 1
    nsub = 4 if H % 4 == 0 else 2 if H % 2 == 0 else 1
    scratch = [
        pltpu.VMEM((db, cb), bf16),
        pltpu.VMEM((tb, cb), bf16),
        pltpu.VMEM((tb, cb), bf16),
        pltpu.VMEM((H, tb, d), bf16),
        pltpu.VMEM((Z, db, cs), bf16),
        pltpu.VMEM((H, tb, cs), bf16),
        pltpu.VMEM((th, cs), f32),
        pltpu.VMEM((8, 128), f32),
        pltpu.VMEM((3, max(X, Y), 8, 128), f32),
        pltpu.VMEM((H, 8, 128), f32),
        pltpu.VMEM((8, 128), f32),
        pltpu.VMEM((3, max(X, Y, Z), 8, 128), f32),
        pltpu.VMEM((2 * H, 128), f32),
        pltpu.VMEM((3, max(X, Y, Z), 2 * H, 128), f32),
        pltpu.VMEM((th, cs), bf16),
        pltpu.VMEM((H, 2, nsub, th // nsub, cs), bf16),
        pltpu.VMEM((2, win, th), bf16),
        pltpu.VMEM((win, cs), f32),
        pltpu.VMEM((db, cb), bf16),
        pltpu.VMEM((2, db, th), f32),
        pltpu.VMEM((nd, X, db // nd, tb), f32),
        pltpu.VMEM((nd, X, db // nd, tb), f32),
        pltpu.VMEM((Y, sub, tb), f32),
        pltpu.VMEM((2, sub, tb), f32),
        pltpu.VMEM((nd, X, db // nd, tb), f32),
        pltpu.VMEM((8, 128), f32),
        pltpu.VMEM((8, 128), f32),
        dma((2,)), dma,
        dma((H,)), dma((H,)),
        dma((2, 2)), dma((2, 2, half)), dma((2, max(X * Y, 2 * X, 2 * Y))),
        dma((Z,)), dma((H,)), dma((Z,)),
        dma((H,)), dma((H,)),
        dma((3,)), dma((3,)),
        dma((H,)), dma((H,)),
        dma((2,)), dma((3,)), dma((H,)),
        dma((3,)), dma((3,)),
        dma((3, nsub)), dma((H, 2, nsub)), dma((H, 2, nsub)),
        dma, dma,
        dma, dma((nd, X)),
        dma, dma((nd,)),
        dma, dma,
        dma, dma,
        dma, dma,
    ]
    vm = pl.BlockSpec(memory_space=pltpu.VMEM)
    hbm = pl.BlockSpec(memory_space=pl.ANY)
    sm = pl.BlockSpec(memory_space=pltpu.SMEM)
    ghead, ghid, stats = pl.pallas_call(
        functools.partial(kernel_body, geo),
        out_shape=(
            jax.ShapeDtypeStruct((db, cb), bf16),
            jax.ShapeDtypeStruct((sub, tb), f32),
            jax.ShapeDtypeStruct((8, 128), f32),
        ),
        in_specs=[hbm, hbm, hbm, sm, sm],
        out_specs=(hbm, vm, vm),
        scratch_shapes=scratch,
        compiler_params=pltpu.CompilerParams(has_side_effects=True, collective_id=0, vmem_limit_bytes=60 * 2**20),
    )(hidden, head, teacher, block_ids, counts)

    def place(
        stats_in, ghid_in, ghead_in, lse_to, kl_to, ghid_to, ghead_to, stats_at, ghid_at, ghead_at, in_sem, out_sem
    ):
        moves = [(stats_in, stats_at), (ghid_in, ghid_at)]
        parts = [pl.ds(k * cs, cs) for k in range(H)]
        moves += [(ghead_in.at[:, part], ghead_at.at[:, part]) for part in parts]
        loads = [pltpu.make_async_copy(src, dst, in_sem.at[k]) for k, (src, dst) in enumerate(moves)]
        for load in loads:
            load.start()
        loads[0].wait()
        stores = [
            pltpu.make_async_copy(stats_at.at[pl.ds(0, 1)], lse_to, out_sem.at[0]),
            pltpu.make_async_copy(stats_at.at[pl.ds(1, 1)], kl_to, out_sem.at[1]),
        ]
        stores[0].start()
        stores[1].start()
        loads[1].wait()
        stores.append(pltpu.make_async_copy(ghid_at, ghid_to, out_sem.at[2]))
        stores[2].start()
        for k, part in enumerate(parts):
            loads[2 + k].wait()
            stores.append(pltpu.make_async_copy(ghead_at.at[:, part], ghead_to.at[:, part], out_sem.at[3 + k]))
            stores[3 + k].start()
        for store in stores:
            store.wait()

    lse, kl, ghid, ghead = pl.pallas_call(
        place,
        out_shape=(
            jax.ShapeDtypeStruct((1, tb), f32),
            jax.ShapeDtypeStruct((1, tb), f32),
            jax.ShapeDtypeStruct(ghid.shape, f32),
            jax.ShapeDtypeStruct(ghead.shape, bf16),
        ),
        in_specs=[hbm, hbm, hbm],
        out_specs=(hbm, hbm, hbm, hbm),
        scratch_shapes=[
            pltpu.VMEM((8, 128), f32),
            pltpu.VMEM(ghid.shape, f32),
            pltpu.VMEM(ghead.shape, bf16),
            dma((2 + H,)),
            dma((3 + H,)),
        ],
    )(stats, ghid, ghead)
    return lse.reshape(tb), kl.reshape(tb), ghid.T, ghead


def solution(mesh, ring_y=RING_Y, blk=BLK):
    vocab, tok = mesh.shape["vocab"], mesh.shape["tok"]
    geo = (vocab // (2 * ring_y), ring_y, tok, blk)
    placed = (P("tok", None), P("tok", "vocab"), P("tok", "vocab"), P("tok", None), P("tok"))
    return jax.shard_map(
        functools.partial(per_device, geo),
        mesh=mesh,
        in_specs=placed,
        out_specs=(P("tok"), P("tok"), P("tok", "vocab"), P("tok", "vocab")),
        check_vma=False,
    )
```
